256 devices in a mesh: seq: 64 (over z, y, x_hi), batch: 4 (over x_lo, core).
Axes of the slice: x: 4 (x_hi: 2, x_lo: 2; x = x_hi * 2 + x_lo), y: 4, z: 8, core: 2. Of those that a mesh axis runs over, the one named last changes fastest.
Arguments:
- queries: bfloat16 [131072, 384], P(('batch', 'seq')), parts along dimension 0, may hold values from -400 to 400
- key_states: bfloat16 [131072, 384], P(('batch', 'seq')), parts along dimension 0, may hold values from -6 to 6
- value_states: bfloat16 [131072, 384], P(('batch', 'seq')), parts along dimension 0, may hold values from -6 to 6
- grad_output: bfloat16 [131072, 384], P(('batch', 'seq')), parts along dimension 0, may hold values from -6 to 6
- partners: int32 [12, 64], P('batch'), parts along dimension 0, may hold values from 0 to 63, each once within a row
- global_blocks: int32 [8], P('batch'), parts along dimension 0, may hold values from 0 to 63
Outputs:
- attended: bfloat16 [131072, 384], P(('batch', 'seq')), parts along dimension 0
- grad_queries: bfloat16 [131072, 384], P(('batch', 'seq')), parts along dimension 0
- grad_keys: bfloat16 [131072, 384], P(('batch', 'seq')), parts along dimension 0
- grad_values: bfloat16 [131072, 384], P(('batch', 'seq')), parts along dimension 0
The draws below stay inside these ranges and needn't reach their ends.
There are 4 independent parts, one for each index of `batch`. The reference program is written for one: setup_inputs(seed, part) draws one part's arguments, and reference() takes and returns one part's arrays. A program takes and returns all parts, laid end to end along the dimension named above; each array names one. Nothing has to cross between parts.
Inputs may be any that keep to these rules, and one draw needn't show every extreme that they name: `partners`: each row names every sequence block once.
All inputs are finite; a program needn't handle non-finite values.
Results may differ from the reference program's by a relative error of at most 0.0065.
Values may be sent and summed in bfloat16 or wider, within the bound.
A program may use at most 128 MiB of HBM per device.

```python
import math
import jax
import jax.numpy as jnp
from jax import lax

BLOCK = 512
HEADS = 6
HD = 64
WIDTH = 384
NB = 64
NT = 32768


def joint_draw(key):
    key_field = jnp.clip(jax.random.normal(jax.random.fold_in(key, 11), (NT, HEADS * HD), jnp.float32), -6.0, 6.0)
    query_field = jnp.clip(2.0 * jax.random.normal(jax.random.fold_in(key, 12), (NT, HEADS * HD), jnp.float32), -12.0, 12.0)
    return (query_field, key_field)


def draw_queries(key, part):
    return joint_draw(key)[0].astype(jnp.bfloat16)


def draw_key_states(key, part):
    return joint_draw(key)[1].astype(jnp.bfloat16)


def shard_levels(own_key, shape, shards, smallest, high):
    level = 1.0
    for axis_at, shards_of in shards:
        draws = jax.random.uniform(jax.random.fold_in(jax.random.fold_in(own_key, 6), axis_at), (shards_of,), jnp.float32, smallest / len(shards), high / len(shards))
        level = level * jnp.repeat(jnp.exp(draws), shape[axis_at] // shards_of).reshape((-1,) + (1,) * (len(shape) - 1 - axis_at))
    return level


def noise(stream_key, extent, deviation, reach, pieces=(), kind=jnp.bfloat16):
    entries = jax.random.normal(stream_key, extent, jnp.float32) * deviation
    if len(pieces) > 0:
        entries = shard_levels(stream_key, extent, pieces, -0.22, 0.18) * entries
    return jnp.clip(entries, min=-reach, max=reach).astype(kind)


def setup_inputs(seed: int = 0, part: int = 0) -> dict:
    key_list = jax.random.split(jax.random.key(seed), 7)
    part_keys = jax.random.split(jax.random.fold_in(key_list[6], part), 7)
    return {
        "queries": draw_queries(jax.random.fold_in(jax.random.fold_in(key_list[6], part), 71), part),
        "key_states": draw_key_states(jax.random.fold_in(jax.random.fold_in(key_list[6], part), 71), part),
        "value_states": noise(part_keys[2], (NT, WIDTH), 1.0, 6.0, ((0, 64),)),
        "grad_output": noise(part_keys[3], (NT, WIDTH), 1.0, 6.0, ((0, 64),)),
        "partners": jax.vmap(lambda own: jax.random.permutation(own, NB))(jax.random.split(part_keys[4], 3)).reshape((3, NB)).astype(jnp.int32),
        "global_blocks": jax.random.randint(part_keys[5], (2,), 0, NB).astype(jnp.int32),
    }


def attend_block(query_rows, key_rows, grad_rows):
    length = key_rows.shape[0]
    scale = 1.0 / math.sqrt(HD)
    highest = lax.Precision.HIGHEST
    query_heads = query_rows.astype(jnp.float32).reshape(BLOCK, HEADS, HD)
    key_heads = key_rows[:, :WIDTH].astype(jnp.float32).reshape(length, HEADS, HD)
    value_heads = key_rows[:, WIDTH:].astype(jnp.float32).reshape(length, HEADS, HD)
    grad_heads = grad_rows.astype(jnp.float32).reshape(BLOCK, HEADS, HD)
    scores = jnp.einsum('qhd,khd->hqk', query_heads, key_heads, precision=highest) * scale
    row_peak = lax.optimization_barrier(jnp.max(scores, axis=-1, keepdims=True))
    exponent = jnp.exp(scores - row_peak)
    weights = exponent / lax.optimization_barrier(jnp.sum(exponent, axis=-1, keepdims=True))
    weights_low = weights.astype(jnp.bfloat16).astype(jnp.float32)
    attended = jnp.einsum('hqk,khd->qhd', weights_low, value_heads, precision=highest)
    attended = attended.reshape(BLOCK, WIDTH).astype(jnp.bfloat16)
    grad_weights = jnp.einsum('qhd,khd->hqk', grad_heads, value_heads, precision=highest)
    row_dots = lax.optimization_barrier(jnp.sum(weights * grad_weights, axis=-1, keepdims=True))
    grad_scores = (weights * (grad_weights - row_dots) * scale).astype(jnp.bfloat16).astype(jnp.float32)
    grad_query = jnp.einsum('hqk,khd->qhd', grad_scores, key_heads, precision=highest)
    grad_query = grad_query.reshape(BLOCK, WIDTH).astype(jnp.bfloat16)
    grad_key = jnp.einsum('hqk,qhd->khd', grad_scores, query_heads, precision=highest).reshape(length, WIDTH)
    grad_value = jnp.einsum('hqk,qhd->khd', weights_low, grad_heads, precision=highest).reshape(length, WIDTH)
    return (attended, grad_query, jnp.concatenate([grad_key, grad_value], axis=1))

def reference(queries, key_states, value_states, grad_output, partners, global_blocks):
    key_value = jnp.concatenate([key_states, value_states], axis=1)
    block_ids = jnp.arange(NB, dtype=jnp.int32)
    route_table = jnp.stack([block_ids, (block_ids - 1) % NB, (block_ids + 1) % NB, partners[0], partners[1], partners[2], jnp.full((NB,), global_blocks[0], jnp.int32), jnp.full((NB,), global_blocks[1], jnp.int32)], axis=1).astype(jnp.int32)

    def visit(grad_total, block_index):
        members = route_table[block_index]
        key_rows = jnp.concatenate([lax.dynamic_slice_in_dim(key_value, (members[position] * BLOCK).astype(jnp.int32), BLOCK, 0) for position in range(8)], axis=0)
        start_row = (block_index * BLOCK).astype(jnp.int32)
        query_rows = lax.dynamic_slice_in_dim(queries, start_row, BLOCK, 0)
        grad_rows = lax.dynamic_slice_in_dim(grad_output, start_row, BLOCK, 0)
        attended, grad_query, grad_pair = attend_block(query_rows, key_rows, grad_rows)
        for position in range(8):
            begin_row = (members[position] * BLOCK).astype(jnp.int32)
            current = lax.dynamic_slice_in_dim(grad_total, begin_row, BLOCK, 0)
            grad_total = lax.dynamic_update_slice_in_dim(grad_total, current + grad_pair[position * BLOCK:(position + 1) * BLOCK], begin_row, 0)
        return (grad_total, (attended, grad_query))
    grad_total, (attended, grad_query) = lax.scan(visit, jnp.zeros((NT, 2 * WIDTH), jnp.float32), block_ids)
    return (attended.reshape(NT, WIDTH), grad_query.reshape(NT, WIDTH), grad_total[:, :WIDTH].astype(jnp.bfloat16), grad_total[:, WIDTH:].astype(jnp.bfloat16))
```

```python
import functools
import math

import jax
import jax.numpy as jnp
from jax import lax
from jax.experimental import pallas as pl
from jax.experimental.pallas import tpu as pltpu
from jax.sharding import PartitionSpec as P

F32 = jnp.float32
BF = jnp.bfloat16
LOG2E = math.log2(math.e)
MESH = pl.DeviceIdType.MESH

PAIRS = 3
BLOCK = 512
SEQ = 64
NZ, NY = 8, 4


def split(device):
    return device // 8, (device // 2) % 4, device % 2


def peers(me, start, stop, body):
    @pl.loop(start, stop)
    def _(k):
        body((me + k) % SEQ)


def remote(src, dst, send, recv, device):
    return pltpu.make_async_remote_copy(
        src_ref=src, dst_ref=dst, send_sem=send, recv_sem=recv, device_id={"seq": device}, device_id_type=MESH
    )


def local(src, dst, sem):
    return pltpu.make_async_copy(src, dst, sem)


def drain(ref, sem):
    pltpu.make_async_copy(ref, ref, sem).wait()


def rows(tiles):
    return tiles.reshape(BLOCK, 128)


def tiles(block):
    return block.reshape(NZ, NY, 16, 128)


def prepare(pair, kv, q_ref, do_ref, kt, vt, qt, qm):
    cols = slice(pair * 128, pair * 128 + 128)
    qs = q_ref[:, cols] * jnp.asarray(0.125, BF)
    lane = lax.broadcasted_iota(jnp.int32, (BLOCK, 128), 1)
    row = lax.broadcasted_iota(jnp.int32, (128, BLOCK), 0)
    qst = qs.T
    for h in range(2):
        qm[h] = jnp.where((lane >= 64) == (h == 1), qs, jnp.zeros_like(qs))
        qt[h] = jnp.where((row >= 64) == (h == 1), qst, jnp.zeros_like(qst))

    @pl.loop(0, 8)
    def _(j):
        kt[j] = rows(kv[pair, 0, j]).T
        t = rows(kv[pair, 1, j]).T
        for h in range(2):
            vt[h, j, 0:64] = t[64 * h : 64 * h + 64]
            vt[h, j, 64:80] = jnp.ones((16, BLOCK), BF)


def head(pair, h, kv, dkv, do_ref, ot, dqt, s_buf, p_buf, kt, vt, qt, qm):
    do_t = do_ref[:, pair * 128 : pair * 128 + 128].astype(F32).T
    qth = qt[h]

    def scores(j, peak):
        s = jnp.dot(rows(kv[pair, 0, j]), qth, preferred_element_type=F32)
        s_buf[j] = s
        return jnp.maximum(peak, jnp.max(s.reshape(BLOCK // 8, 8, BLOCK), axis=0))

    peak = lax.fori_loop(0, 8, scores, jnp.full((8, BLOCK), -jnp.inf, F32))
    peak = jnp.max(peak, axis=0, keepdims=True) * LOG2E

    def weigh(j, acc):
        p = jnp.exp2(s_buf[j] * LOG2E - peak).astype(BF)
        p_buf[j] = p
        return acc + jnp.dot(vt[h, j], p, preferred_element_type=F32)

    acc = lax.fori_loop(0, 8, weigh, jnp.zeros((80, BLOCK), F32))
    inverse = 1.0 / acc[64:65]
    out = acc[0:64] * inverse
    ot[64 * h : 64 * h + 64] = out
    do_n = (do_t[64 * h : 64 * h + 64] * inverse).astype(BF)
    dots = jnp.sum(do_n.astype(F32) * out, axis=0, keepdims=True)
    zero = jnp.zeros((64, BLOCK), BF)
    do_full = jnp.concatenate([do_n, zero] if h == 0 else [zero, do_n], axis=0)
    do_rows = do_full.T
    qmh = qm[h]

    def backward(j, acc):
        p = p_buf[j]
        gw = jnp.dot(rows(kv[pair, 1, j]), do_full, preferred_element_type=F32)
        ds = (p.astype(F32) * (gw - dots)).astype(BF)
        dk = jnp.dot(ds, qmh, preferred_element_type=F32).astype(BF)
        dv = jnp.dot(p, do_rows, preferred_element_type=F32).astype(BF)
        if h == 0:
            dkv[pair, 0, j] = tiles(dk)
            dkv[pair, 1, j] = tiles(dv)
        else:
            dkv[pair, 0, j] = dkv[pair, 0, j] + tiles(dk)
            dkv[pair, 1, j] = dkv[pair, 1, j] + tiles(dv)
        return acc + jnp.dot(kt[j, 64 * h : 64 * h + 64], ds, preferred_element_type=F32)

    dq = lax.fori_loop(0, 8, backward, jnp.zeros((64, BLOCK), F32))
    dqt[64 * h : 64 * h + 64] = dq * 0.125


def kernel(
    table, inverse, hot, q_ref, do_ref, k_ref, v_ref, o_ref, dq_ref, gk_ref, gv_ref,
    kv, dkv, spread, picked, gsel, coming0, coming1, coming2, near, rsy, ysum, rsx, xsum, rsz, ret, retin,
    s_buf, p_buf, kt, vt, qt, qm, ot, dqt,
    load_sem, own_sem, p1_send, p1_recv, p2_send, p2_recv, nb_send, nb_recv,
    gz_send, gz_recv, gx_send, gx_recv, gy_send, gy_recv,
    b1_send, b1_recv, bn_send, bn_recv, ry_send, ry_recv, rx_send, rx_recv, rz_send, rz_recv, b2_send, b2_recv,
):
    coming = (coming0, coming1, coming2)
    me = lax.axis_index("seq")
    z, y, x = split(me)
    right, left = (me + 1) % SEQ, (me + SEQ - 1) % SEQ

    loads = []
    for pair in range(PAIRS):
        for which, ref in enumerate((k_ref, v_ref)):
            loads.append(local(ref.at[:, :, :, pair * 128 : pair * 128 + 128], kv.at[pair, which, 0], load_sem.at[pair, which]))
    for copy in loads:
        copy.start()

    barrier = pltpu.get_barrier_semaphore()

    def hello(device):
        pl.semaphore_signal(barrier, inc=1, device_id={"seq": device}, device_id_type=MESH)

    peers(me, 1, SEQ, hello)
    pl.semaphore_wait(barrier, SEQ - 1)
    for copy in loads:
        copy.wait()

    def scatter(d):
        dz, dy, dx = split(d)
        remote(kv.at[:, dx, 0, dz, dy], spread.at[me], p1_send, p1_recv, d).start()

    own = local(kv.at[:, x, 0, z, y], spread.at[me], own_sem.at[0])
    own.start()
    peers(me, 1, SEQ, scatter)

    def neighbours(pair):
        return [
            remote(kv.at[pair, :, 0], kv.at[pair, :, 1], nb_send.at[pair, 0], nb_recv.at[pair, 0], right),
            remote(kv.at[pair, :, 0], kv.at[pair, :, 2], nb_send.at[pair, 1], nb_recv.at[pair, 1], left),
        ]

    def start_neighbours(pair):
        for copy in neighbours(pair):
            copy.start()

    start_neighbours(0)
    own.wait()
    drain(spread.at[pl.ds(0, SEQ - 1)], p1_recv)

    for g in range(2):
        gsel[:, g] = spread[table[3 + g, 0]]
    own_g = local(gsel, kv.at[:, x, 6:8, z, y], own_sem.at[1])
    own_g.start()

    @pl.loop(1, NZ)
    def _(k):
        d = ((z + k) % NZ) * 8 + y * 2 + x
        remote(gsel, kv.at[:, x, 6:8, z, y], gz_send, gz_recv, d).start()

    def pick(pair):
        @pl.loop(0, SEQ)
        def _(d):
            for r in range(3):
                picked[pair, d, r] = spread[table[r, d], pair]

    def start_routes(pair):
        local(picked.at[pair, me], kv.at[pair, x, 3:6, z, y], own_sem.at[2 + pair]).start()

        def send(d):
            remote(picked.at[pair, d], kv.at[pair, x, 3:6, z, y], p2_send.at[pair], p2_recv.at[pair], d).start()

        peers(me, 1, SEQ, send)

    pick(0)
    start_routes(0)
    own_g.wait()
    drain(kv.at[:, x, 6:8, 0 : NZ - 1, y], gz_recv)
    across = [
        remote(kv.at[pair, x, 6:8, :, y], kv.at[pair, x, 6:8, :, y], gx_send.at[pair], gx_recv.at[pair], z * 8 + y * 2 + 1 - x)
        for pair in range(PAIRS)
    ]
    for copy in across:
        copy.start()
    pick(1)
    pick(2)
    for pair in range(PAIRS):
        across[pair].wait_recv()

        @pl.loop(1, NY)
        def _(k):
            d = z * 8 + ((y + k) % NY) * 2 + x
            remote(kv.at[pair, :, 6:8, :, y], kv.at[pair, :, 6:8, :, y], gy_send.at[pair], gy_recv.at[pair], d).start()

    for pair in range(1, PAIRS):
        start_neighbours(pair)
        start_routes(pair)

    def arrive(pair):
        for copy in neighbours(pair):
            copy.wait_recv()
        local(picked.at[pair, me], kv.at[pair, x, 3:6, z, y], own_sem.at[2 + pair]).wait()
        drain(picked.at[pair, pl.ds(0, SEQ - 1)], p2_recv.at[pair])
        drain(kv.at[pair, :, 6:8, :, 0 : NY - 1], gy_recv.at[pair])

    def back_neighbours(pair):
        return [
            remote(dkv.at[pair, :, 1], near.at[pair, 0], bn_send.at[pair, 0], bn_recv.at[pair, 0], left),
            remote(dkv.at[pair, :, 2], near.at[pair, 1], bn_send.at[pair, 1], bn_recv.at[pair, 1], right),
        ]

    def back_own(pair):
        return local(dkv.at[pair, x, 3:6, z, y], coming[pair].at[me], own_sem.at[5 + pair])

    def stage0(pair):
        for k in range(1, NY):
            to = (y + k) % NY
            remote(
                dkv.at[pair, :, 6:8, :, to], rsy.at[pair, k - 1], ry_send.at[pair, k - 1], ry_recv.at[pair, k - 1],
                z * 8 + to * 2 + x,
            ).start()
        back_own(pair).start()

        def send(d):
            dz, dy, dx = split(d)
            remote(dkv.at[pair, dx, 3:6, dz, dy], coming[pair].at[me], b1_send.at[pair], b1_recv.at[pair], d).start()

        peers(me, 1, SEQ, send)
        for copy in back_neighbours(pair):
            copy.start()

    def stage1_copy(pair):
        return remote(ysum.at[pair, 1 - x], rsx.at[pair], rx_send.at[pair], rx_recv.at[pair], z * 8 + y * 2 + 1 - x)

    def stage1(pair):
        for k in range(1, NY):
            drain(rsy.at[pair, k - 1], ry_recv.at[pair, k - 1])
        for which in range(2):
            total = dkv[pair, which, 6:8, :, y].astype(F32)
            for k in range(NY - 1):
                total = total + rsy[pair, k, which].astype(F32)
            ysum[pair, which] = total.astype(BF)
        stage1_copy(pair).start()

    def stage2(pair):
        stage1_copy(pair).wait_recv()
        xsum[pair] = (ysum[pair, x].astype(F32) + rsx[pair].astype(F32)).astype(BF)
        for k in range(1, NZ):
            to = (z + k) % NZ
            remote(
                xsum.at[pair, :, to], rsz.at[pair, k - 1], rz_send.at[pair, k - 1], rz_recv.at[pair, k - 1],
                to * 8 + y * 2 + x,
            ).start()

    def stage3(pair):
        for k in range(1, NZ):
            drain(rsz.at[pair, k - 1], rz_recv.at[pair, k - 1])
        shared = xsum[pair, :, z].astype(F32)
        for k in range(NZ - 1):
            shared = shared + rsz[pair, k].astype(F32)
        back_own(pair).wait()
        drain(coming[pair].at[pl.ds(0, SEQ - 1)], b1_recv.at[pair])

        @pl.loop(0, SEQ)
        def _(c):
            total = hot[0, c] * shared[0] + hot[1, c] * shared[1]
            for r in range(3):
                total = total + coming[pair][inverse[r, c], r].astype(F32)
            ret[pair, c] = total.astype(BF)

        local(ret.at[pair, me], retin.at[pair, x, z, y], own_sem.at[8 + pair]).start()

        def send(d):
            remote(ret.at[pair, d], retin.at[pair, x, z, y], b2_send.at[pair], b2_recv.at[pair], d).start()

        peers(me, 1, SEQ, send)

    def stage4(pair):
        for copy in back_neighbours(pair):
            copy.wait_recv()
        local(ret.at[pair, me], retin.at[pair, x, z, y], own_sem.at[8 + pair]).wait()
        drain(ret.at[pair, pl.ds(0, SEQ - 1)], b2_recv.at[pair])
        for which, ref in enumerate((gk_ref, gv_ref)):
            total = dkv[pair, which, 0].astype(F32) + retin[pair, which].astype(F32)
            total = total + near[pair, 0, which].astype(F32) + near[pair, 1, which].astype(F32)
            ref[:, pair * 128 : pair * 128 + 128] = rows(total.astype(BF))

    def begin(pair):
        arrive(pair)
        prepare(pair, kv, q_ref, do_ref, kt, vt, qt, qm)

    def half(pair, h):
        head(pair, h, kv, dkv, do_ref, ot, dqt, s_buf, p_buf, kt, vt, qt, qm)

    def finish(pair):
        cols = slice(pair * 128, pair * 128 + 128)
        o_ref[:, cols] = ot[...].T.astype(BF)
        dq_ref[:, cols] = dqt[...].T.astype(BF)

    begin(0)
    half(0, 0)
    half(0, 1)
    stage0(0)
    finish(0)
    begin(1)
    half(1, 0)
    stage1(0)
    half(1, 1)
    stage0(1)
    stage2(0)
    finish(1)
    begin(2)
    half(2, 0)
    stage3(0)
    stage1(1)
    half(2, 1)
    stage0(2)
    stage2(1)
    finish(2)
    stage1(2)
    stage3(1)
    stage2(2)
    stage4(0)
    stage3(2)
    stage4(1)
    stage4(2)

    drain(spread.at[pl.ds(0, SEQ - 1)], p1_send)
    drain(kv.at[:, x, 6:8, 0 : NZ - 1, y], gz_send)
    for pair in range(PAIRS):
        for copy in neighbours(pair) + back_neighbours(pair):
            copy.wait_send()
        drain(picked.at[pair, pl.ds(0, SEQ - 1)], p2_send.at[pair])
        across[pair].wait_send()
        drain(kv.at[pair, :, 6:8, :, 0 : NY - 1], gy_send.at[pair])
        drain(coming[pair].at[pl.ds(0, SEQ - 1)], b1_send.at[pair])
        for k in range(NY - 1):
            drain(rsy.at[pair, k], ry_send.at[pair, k])
        stage1_copy(pair).wait_send()
        for k in range(NZ - 1):
            drain(rsz.at[pair, k], rz_send.at[pair, k])
        drain(ret.at[pair, pl.ds(0, SEQ - 1)], b2_send.at[pair])


def step(queries, key_states, value_states, grad_output, partners, global_blocks):
    ids = jnp.arange(SEQ, dtype=jnp.int32)
    table = jnp.concatenate([partners, jnp.broadcast_to(global_blocks[:, None], (2, SEQ))], axis=0)
    inverse = jnp.sum(jnp.where(partners[:, :, None] == ids[None, None, :], ids[None, :, None], 0), axis=1)
    hot = (global_blocks[:, None] == ids[None, :]).astype(F32)
    vmem = pl.BlockSpec(memory_space=pltpu.VMEM)
    smem = pl.BlockSpec(memory_space=pltpu.SMEM)
    anywhere = pl.BlockSpec(memory_space=pl.ANY)
    scratch = [
        pltpu.VMEM((PAIRS, 2, 8, NZ, NY, 16, 128), BF),
        pltpu.VMEM((PAIRS, 2, 8, NZ, NY, 16, 128), BF),
        pltpu.VMEM((SEQ, PAIRS, 16, 128), BF),
        pltpu.VMEM((PAIRS, SEQ, 3, 16, 128), BF),
        pltpu.VMEM((PAIRS, 2, 16, 128), BF),
        pltpu.VMEM((SEQ, 3, 16, 128), BF),
        pltpu.VMEM((SEQ, 3, 16, 128), BF),
        pltpu.VMEM((SEQ, 3, 16, 128), BF),
        pltpu.VMEM((PAIRS, 2, 2, NZ, NY, 16, 128), BF),
        pltpu.VMEM((PAIRS, NY - 1, 2, 2, NZ, 16, 128), BF),
        pltpu.VMEM((PAIRS, 2, 2, NZ, 16, 128), BF),
        pltpu.VMEM((PAIRS, 2, NZ, 16, 128), BF),
        pltpu.VMEM((PAIRS, 2, NZ, 16, 128), BF),
        pltpu.VMEM((PAIRS, NZ - 1, 2, 16, 128), BF),
        pltpu.VMEM((PAIRS, SEQ, 16, 128), BF),
        pltpu.VMEM((PAIRS, 2, NZ, NY, 16, 128), BF),
        pltpu.VMEM((8, BLOCK, BLOCK), F32),
        pltpu.VMEM((8, BLOCK, BLOCK), BF),
        pltpu.VMEM((8, 128, BLOCK), BF),
        pltpu.VMEM((2, 8, 80, BLOCK), BF),
        pltpu.VMEM((2, 128, BLOCK), BF),
        pltpu.VMEM((2, BLOCK, 128), BF),
        pltpu.VMEM((128, BLOCK), F32),
        pltpu.VMEM((128, BLOCK), F32),
    ]
    dma = pltpu.SemaphoreType.DMA
    sems = [
        dma((PAIRS, 2)), dma((11,)), dma(()), dma(()), dma((PAIRS,)), dma((PAIRS,)), dma((PAIRS, 2)), dma((PAIRS, 2)),
        dma(()), dma(()), dma((PAIRS,)), dma((PAIRS,)), dma((PAIRS,)), dma((PAIRS,)),
        dma((PAIRS,)), dma((PAIRS,)), dma((PAIRS, 2)), dma((PAIRS, 2)),
        dma((PAIRS, NY - 1)), dma((PAIRS, NY - 1)), dma((PAIRS,)), dma((PAIRS,)),
        dma((PAIRS, NZ - 1)), dma((PAIRS, NZ - 1)), dma((PAIRS,)), dma((PAIRS,)),
    ]
    grid_rows = (NZ, NY, 16, PAIRS * 128)
    return pl.pallas_call(
        kernel,
        out_shape=tuple(jax.ShapeDtypeStruct((BLOCK, PAIRS * 128), BF) for _ in range(4)),
        in_specs=[smem, smem, smem, vmem, vmem, anywhere, anywhere],
        out_specs=(vmem,) * 4,
        scratch_shapes=scratch + sems,
        compiler_params=pltpu.CompilerParams(
            collective_id=0, has_side_effects=True, vmem_limit_bytes=60 * 1024 * 1024
        ),
    )(table, inverse, hot, queries, grad_output, key_states.reshape(grid_rows), value_states.reshape(grid_rows))


def solution(mesh):
    spec = P(("batch", "seq"), None)
    return jax.shard_map(
        step,
        mesh=mesh,
        in_specs=(spec, spec, spec, spec, P("batch", None), P("batch")),
        out_specs=(spec,) * 4,
        check_vma=False,
    )
```

```python
import functools
import math

import jax
import jax.numpy as jnp
from jax import lax
from jax.experimental import pallas as pl
from jax.experimental.pallas import tpu as pltpu
from jax.sharding import PartitionSpec as P

F32 = jnp.float32
BF = jnp.bfloat16
LOG2E = math.log2(math.e)
MESH = pl.DeviceIdType.MESH

PAIRS = 3
BLOCK = 512
SEQ = 64
NZ, NY = 8, 4
EDGES = 16


def split(device):
    return device // 8, (device // 2) % 4, device % 2


def peers(me, start, stop, body):
    @pl.loop(start, stop)
    def _(k):
        body((me + k) % SEQ)


def remote(src, dst, send, recv, device):
    return pltpu.make_async_remote_copy(
        src_ref=src, dst_ref=dst, send_sem=send, recv_sem=recv, device_id={"seq": device}, device_id_type=MESH
    )


def local(src, dst, sem):
    return pltpu.make_async_copy(src, dst, sem)


def drain(ref, sem):
    pltpu.make_async_copy(ref, ref, sem).wait()


def edge_device(e):
    return (8 * (e // 2) + SEQ - 1 + e % 2) % SEQ


def edge_block(e):
    return (8 * (e // 2) + SEQ - e % 2) % SEQ


def rows(tiles):
    return tiles.reshape(BLOCK, 128)


def tiles(block):
    return block.reshape(NZ, NY, 16, 128)


def prepare(pair, kv, q_ref, do_ref, kt, vt, qt, qm):
    cols = slice(pair * 128, pair * 128 + 128)
    qs = q_ref[:, cols] * jnp.asarray(0.125, BF)
    lane = lax.broadcasted_iota(jnp.int32, (BLOCK, 128), 1)
    row = lax.broadcasted_iota(jnp.int32, (128, BLOCK), 0)
    qst = qs.T
    for h in range(2):
        qm[h] = jnp.where((lane >= 64) == (h == 1), qs, jnp.zeros_like(qs))
        qt[h] = jnp.where((row >= 64) == (h == 1), qst, jnp.zeros_like(qst))

    @pl.loop(0, 8)
    def _(j):
        kt[j] = rows(kv[pair, 0, j]).T
        t = rows(kv[pair, 1, j]).T
        for h in range(2):
            vt[h, j, 0:64] = t[64 * h : 64 * h + 64]
            vt[h, j, 64:80] = jnp.ones((16, BLOCK), BF)


def head(pair, h, ticks, kv, dkv, do_ref, ot, dqt, s_buf, p_buf, kt, vt, qt, qm):
    do_t = do_ref[:, pair * 128 : pair * 128 + 128].astype(F32).T
    qth = qt[h]

    def scores(j, peak):
        s = jnp.dot(rows(kv[pair, 0, j]), qth, preferred_element_type=F32)
        s_buf[j] = s
        return jnp.maximum(peak, jnp.max(s.reshape(BLOCK // 8, 8, BLOCK), axis=0))

    peak = lax.fori_loop(0, 8, scores, jnp.full((8, BLOCK), -jnp.inf, F32))
    peak = jnp.max(peak, axis=0, keepdims=True) * LOG2E
    ticks[0]()

    def weigh(j, acc):
        p = jnp.exp2(s_buf[j] * LOG2E - peak).astype(BF)
        p_buf[j] = p
        return acc + jnp.dot(vt[h, j], p, preferred_element_type=F32)

    acc = lax.fori_loop(0, 8, weigh, jnp.zeros((80, BLOCK), F32))
    inverse = 1.0 / acc[64:65]
    out = acc[0:64] * inverse
    ot[64 * h : 64 * h + 64] = out
    do_n = (do_t[64 * h : 64 * h + 64] * inverse).astype(BF)
    dots = jnp.sum(do_n.astype(F32) * out, axis=0, keepdims=True)
    zero = jnp.zeros((64, BLOCK), BF)
    do_full = jnp.concatenate([do_n, zero] if h == 0 else [zero, do_n], axis=0)
    do_rows = do_full.T
    qmh = qm[h]
    ticks[1]()

    def backward(j, acc):
        p = p_buf[j]
        gw = jnp.dot(rows(kv[pair, 1, j]), do_full, preferred_element_type=F32)
        ds = (p.astype(F32) * (gw - dots)).astype(BF)
        dk = jnp.dot(ds, qmh, preferred_element_type=F32).astype(BF)
        dv = jnp.dot(p, do_rows, preferred_element_type=F32).astype(BF)
        if h == 0:
            dkv[pair, 0, j] = tiles(dk)
            dkv[pair, 1, j] = tiles(dv)
        else:
            dkv[pair, 0, j] = dkv[pair, 0, j] + tiles(dk)
            dkv[pair, 1, j] = dkv[pair, 1, j] + tiles(dv)
        return acc + jnp.dot(kt[j, 64 * h : 64 * h + 64], ds, preferred_element_type=F32)

    dq = lax.fori_loop(0, 8, backward, jnp.zeros((64, BLOCK), F32))
    dqt[64 * h : 64 * h + 64] = dq * 0.125


def kernel(
    table, inverse, shared_ids, q_ref, do_ref, k_ref, v_ref, o_ref, dq_ref, gk_ref, gv_ref,
    kv, dkv, spread0, spread1, spread2, picked, gsel, coming0, coming1, coming2, extra0, extra1, extra2, far_in, near_out, near_in,
    rsy, ysum, rsx, xsum, rsz, ret, retin,
    s_buf, p_buf, kt, vt, qt, qm, ot, dqt,
    load_sem, own_sem, p1_send, p1_recv, p2_send, p2_recv, na_send, na_recv, nf_send, nf_recv,
    gz_send, gz_recv, gx_send, gx_recv, gy_send, gy_recv,
    b1_send, b1_recv, bf_send, bf_recv, bn_send, bn_recv,
    pc_send, pc_recv, bc_send, bc_recv,
    ry_send, ry_recv, rx_send, rx_recv, rz_send, rz_recv, b2_send, b2_recv,
):
    spread = (spread0, spread1, spread2)
    coming = (coming0, coming1, coming2)
    extra = (extra0, extra1, extra2)
    me = lax.axis_index("seq")
    z, y, x = split(me)
    twin = z * 8 + y * 2 + 1 - x
    up = (me + 2) % SEQ
    down = (me + SEQ - 2) % SEQ
    ahead = up * (1 - x) + down * x
    behind = down * (1 - x) + up * x
    near = 2 - x
    far = 1 + x
    edge = y == 3 * x
    inner = y != 3 * x
    hands = y != 3 - 3 * x
    place = (2 * z + 1 + x) % EDGES

    def scoped(name):
        return jax.named_scope(name)

    def loads(pair):
        return [
            local(ref.at[:, :, :, pair * 128 : pair * 128 + 128], kv.at[pair, which, 0], load_sem.at[pair, which])
            for which, ref in enumerate((k_ref, v_ref))
        ]

    for pair in range(PAIRS):
        for copy in loads(pair):
            copy.start()

    barrier = pltpu.get_barrier_semaphore()

    def hello(device):
        pl.semaphore_signal(barrier, inc=1, device_id={"seq": device}, device_id_type=MESH)

    with scoped("barrier"):
        peers(me, 1, SEQ, hello)
        pl.semaphore_wait(barrier, SEQ - 1)

    def keep_own(pair):
        return local(kv.at[pair, x, 0, z, y], spread[pair].at[me], own_sem.at[pair])

    def keep(pair):
        for copy in loads(pair):
            copy.wait()
        keep_own(pair).start()

        def send(d):
            dz, dy, dx = split(d)
            remote(kv.at[pair, dx, 0, dz, dy], spread[pair].at[me], p1_send.at[pair], p1_recv.at[pair], d).start()

        peers(me, 1, SEQ, send)

    def kept(pair):
        keep_own(pair).wait()
        drain(spread[pair].at[pl.ds(0, SEQ - 1)], p1_recv.at[pair])

    def to_twin(pair):
        return remote(kv.at[pair, :, 0], kv.at[pair, :, 3 - near], na_send.at[pair], na_recv.at[pair], twin)

    def to_next(pair):
        return remote(kv.at[pair, :, near], kv.at[pair, :, 3 - near], nf_send.at[pair], nf_recv.at[pair], ahead)

    def hand_on(pair):
        to_twin(pair).wait_recv()

        @pl.when(hands)
        def _():
            to_next(pair).start()

    def edge_own(pair):
        mate = edge_block(place)
        return local(spread[pair].at[mate], kv.at[pair, x, far, z, y], own_sem.at[15 + pair])

    def edges(pair):
        @pl.loop(0, EDGES)
        def _(e):
            d = edge_device(e)

            @pl.when(d != me)
            def _():
                remote(
                    spread[pair].at[edge_block(e)], kv.at[pair, x, 2 - e % 2, z, y], pc_send.at[pair], pc_recv.at[pair], d
                ).start()

        @pl.when(edge)
        def _():
            edge_own(pair).start()

    def global_own(pair):
        return local(gsel.at[pair], kv.at[pair, x, 6:8, z, y], own_sem.at[3 + pair])

    def global_z(pair):
        for g in range(2):
            gsel[pair, g] = spread[pair][shared_ids[g]]
        global_own(pair).start()

        @pl.loop(1, NZ)
        def _(k):
            d = ((z + k) % NZ) * 8 + y * 2 + x
            remote(gsel.at[pair], kv.at[pair, x, 6:8, z, y], gz_send.at[pair], gz_recv.at[pair], d).start()

    def across(pair):
        return remote(
            kv.at[pair, x, 6:8, :, y], kv.at[pair, x, 6:8, :, y], gx_send.at[pair], gx_recv.at[pair], twin
        )

    def global_x(pair):
        global_own(pair).wait()
        drain(kv.at[pair, x, 6:8, 0 : NZ - 1, y], gz_recv.at[pair])
        across(pair).start()

    def global_y(pair):
        across(pair).wait_recv()

        @pl.loop(1, NY)
        def _(k):
            d = z * 8 + ((y + k) % NY) * 2 + x
            remote(kv.at[pair, :, 6:8, :, y], kv.at[pair, :, 6:8, :, y], gy_send.at[pair], gy_recv.at[pair], d).start()

    def pick(pair):
        @pl.loop(0, SEQ)
        def _(d):
            for r in range(3):
                picked[pair, d, r] = spread[pair][table[r, d]]

    def route_own(pair):
        return local(picked.at[pair, me], kv.at[pair, x, 3:6, z, y], own_sem.at[6 + pair])

    def routes(pair):
        route_own(pair).start()

        def send(d):
            remote(picked.at[pair, d], kv.at[pair, x, 3:6, z, y], p2_send.at[pair], p2_recv.at[pair], d).start()

        peers(me, 1, SEQ, send)

    def arrive(pair):
        with scoped("arrive_nb%d" % pair):
            @pl.when(inner)
            def _():
                to_next(pair).wait_recv()

            @pl.when(edge)
            def _():
                edge_own(pair).wait()
                drain(spread[pair].at[pl.ds(0, SEQ - 1)], pc_recv.at[pair])
        with scoped("arrive_p2_%d" % pair):
            route_own(pair).wait()
            drain(picked.at[pair, pl.ds(0, SEQ - 1)], p2_recv.at[pair])
        with scoped("arrive_g%d" % pair):
            drain(kv.at[pair, :, 6:8, :, 0 : NY - 1], gy_recv.at[pair])

    def back_far(pair):
        return remote(dkv.at[pair, :, far], far_in.at[pair], bf_send.at[pair], bf_recv.at[pair], behind)

    def back_near(pair):
        return remote(near_out.at[pair], near_in.at[pair], bn_send.at[pair], bn_recv.at[pair], twin)

    def back_own(pair):
        return local(dkv.at[pair, x, 3:6, z, y], coming[pair].at[me], own_sem.at[9 + pair])

    def ret_own(pair):
        return local(ret.at[pair, me], retin.at[pair, x, z, y], own_sem.at[12 + pair])

    def edge_back_own(pair):
        return local(dkv.at[pair, x, far, z, y], extra[pair].at[place], own_sem.at[18 + pair])

    def stage0(pair):
        for k in range(1, NY):
            to = (y + k) % NY
            remote(
                dkv.at[pair, :, 6:8, :, to], rsy.at[pair, k - 1], ry_send.at[pair, k - 1], ry_recv.at[pair, k - 1],
                z * 8 + to * 2 + x,
            ).start()
        @pl.when(inner)
        def _():
            back_far(pair).start()

        @pl.when(edge)
        def _():
            edge_back_own(pair).start()

            def send_edge(d):
                dz, dy, dx = split(d)
                remote(dkv.at[pair, dx, far, dz, dy], extra[pair].at[place], bc_send.at[pair], bc_recv.at[pair], d).start()

            peers(me, 1, SEQ, send_edge)

        back_own(pair).start()

        def send(d):
            dz, dy, dx = split(d)
            remote(dkv.at[pair, dx, 3:6, dz, dy], coming[pair].at[me], b1_send.at[pair], b1_recv.at[pair], d).start()

        peers(me, 1, SEQ, send)

    def back_x(pair):
        return remote(ysum.at[pair, 1 - x], rsx.at[pair], rx_send.at[pair], rx_recv.at[pair], twin)

    def stage1(pair):
        for k in range(1, NY):
            drain(rsy.at[pair, k - 1], ry_recv.at[pair, k - 1])
        for which in range(2):
            total = dkv[pair, which, 6:8, :, y].astype(F32)
            for k in range(NY - 1):
                total = total + rsy[pair, k, which].astype(F32)
            ysum[pair, which] = total.astype(BF)
        back_x(pair).start()

    def relay(pair):
        @pl.when(hands)
        def _():
            back_far(pair).wait_recv()
            for which in range(2):
                total = dkv[pair, which, near].astype(F32) + far_in[pair, which].astype(F32)
                near_out[pair, which] = total.astype(BF)

        @pl.when(y == 3 - 3 * x)
        def _():
            for which in range(2):
                near_out[pair, which] = dkv[pair, which, near]

        back_near(pair).start()

    def stage2(pair):
        back_x(pair).wait_recv()
        xsum[pair] = (ysum[pair, x].astype(F32) + rsx[pair].astype(F32)).astype(BF)
        for k in range(1, NZ):
            to = (z + k) % NZ
            remote(
                xsum.at[pair, :, to], rsz.at[pair, k - 1], rz_send.at[pair, k - 1], rz_recv.at[pair, k - 1],
                to * 8 + y * 2 + x,
            ).start()

    def stage3(pair):
        for k in range(1, NZ):
            drain(rsz.at[pair, k - 1], rz_recv.at[pair, k - 1])
        shared = xsum[pair, :, z].astype(F32)
        for k in range(NZ - 1):
            shared = shared + rsz[pair, k].astype(F32)
        back_own(pair).wait()
        drain(coming[pair].at[pl.ds(0, SEQ - 1)], b1_recv.at[pair])

        @pl.when(edge)
        def _():
            edge_back_own(pair).wait()
            drain(extra[pair].at[pl.ds(0, EDGES - 1)], bc_recv.at[pair])

        @pl.when(inner)
        def _():
            drain(extra[pair], bc_recv.at[pair])

        def total_of(c):
            total = sum((shared_ids[g] == c).astype(F32) * shared[g] for g in range(2))
            for r in range(3):
                total = total + coming[pair][inverse[r, c], r].astype(F32)
            return total

        @pl.loop(0, SEQ)
        def _(c):
            ret[pair, c] = total_of(c).astype(BF)

        @pl.loop(0, EDGES)
        def _(e):
            c = edge_block(e)
            ret[pair, c] = (total_of(c) + extra[pair][e].astype(F32)).astype(BF)

        ret_own(pair).start()

        def send(d):
            remote(ret.at[pair, d], retin.at[pair, x, z, y], b2_send.at[pair], b2_recv.at[pair], d).start()

        peers(me, 1, SEQ, send)

    def stage4(pair):
        back_near(pair).wait_recv()
        ret_own(pair).wait()
        drain(ret.at[pair, pl.ds(0, SEQ - 1)], b2_recv.at[pair])
        for which, ref in enumerate((gk_ref, gv_ref)):
            total = dkv[pair, which, 0].astype(F32) + retin[pair, which].astype(F32) + near_in[pair, which].astype(F32)
            ref[:, pair * 128 : pair * 128 + 128] = rows(total.astype(BF))

    def finish(pair):
        cols = slice(pair * 128, pair * 128 + 128)
        o_ref[:, cols] = ot[...].T.astype(BF)
        dq_ref[:, cols] = dqt[...].T.astype(BF)

    def run(work):
        for stage, pair in work:
            with scoped("%s_%d" % (stage.__name__, pair)):
                stage(pair)

    def compute(pair, *work):
        arrive(pair)
        prepare(pair, kv, q_ref, do_ref, kt, vt, qt, qm)
        for h in range(2):
            ticks = [functools.partial(run, work[3 * h + i]) for i in range(3)]
            head(pair, h, ticks, kv, dkv, do_ref, ot, dqt, s_buf, p_buf, kt, vt, qt, qm)
            ticks[2]()
        with scoped("stage0_%d" % pair):
            stage0(pair)
        finish(pair)

    def to_twin_start(pair):
        to_twin(pair).start()

    run([(keep, 0), (keep, 1), (keep, 2), (to_twin_start, 0), (to_twin_start, 1), (to_twin_start, 2)])
    run([(kept, 0), (global_z, 0), (kept, 1), (global_z, 1), (kept, 2), (global_z, 2), (pick, 0), (edges, 0), (routes, 0)])
    run([(hand_on, 0), (global_x, 0), (global_x, 1), (global_x, 2), (pick, 1), (pick, 2), (hand_on, 1)])
    run([(global_y, 0), (edges, 1), (routes, 1), (hand_on, 2), (global_y, 1), (edges, 2), (routes, 2), (global_y, 2)])
    compute(0, [], [], [], [], [], [])
    compute(1, [], [], [], [], [(stage1, 0)], [(stage2, 0)])
    compute(2, [(relay, 0)], [], [], [(stage3, 0)], [(stage1, 1)], [(stage2, 1)])
    run([(relay, 1), (stage1, 2), (stage3, 1), (stage2, 2), (stage4, 0), (relay, 2), (stage3, 2), (stage4, 1), (stage4, 2)])

    for pair in range(PAIRS):
        drain(spread[pair].at[pl.ds(0, SEQ - 1)], p1_send.at[pair])
        drain(kv.at[pair, x, 6:8, 0 : NZ - 1, y], gz_send.at[pair])
        for copy in (to_twin(pair), across(pair), back_near(pair), back_x(pair)):
            copy.wait_send()

        @pl.when(hands)
        def _():
            to_next(pair).wait_send()

        @pl.when(inner)
        def _():
            back_far(pair).wait_send()
            drain(extra[pair], pc_send.at[pair])

        @pl.when(edge)
        def _():
            drain(extra[pair].at[pl.ds(0, EDGES - 1)], pc_send.at[pair])
            drain(spread[pair].at[pl.ds(0, SEQ - 1)], bc_send.at[pair])

        drain(picked.at[pair, pl.ds(0, SEQ - 1)], p2_send.at[pair])
        drain(kv.at[pair, :, 6:8, :, 0 : NY - 1], gy_send.at[pair])
        drain(coming[pair].at[pl.ds(0, SEQ - 1)], b1_send.at[pair])
        for k in range(NY - 1):
            drain(rsy.at[pair, k], ry_send.at[pair, k])
        for k in range(NZ - 1):
            drain(rsz.at[pair, k], rz_send.at[pair, k])
        drain(ret.at[pair, pl.ds(0, SEQ - 1)], b2_send.at[pair])


def step(queries, key_states, value_states, grad_output, partners, global_blocks):
    ids = jnp.arange(SEQ, dtype=jnp.int32)
    inverse = jnp.sum(jnp.where(partners[:, :, None] == ids[None, None, :], ids[None, :, None], 0), axis=1)
    vmem = pl.BlockSpec(memory_space=pltpu.VMEM)
    smem = pl.BlockSpec(memory_space=pltpu.SMEM)
    anywhere = pl.BlockSpec(memory_space=pl.ANY)
    scratch = [
        pltpu.VMEM((PAIRS, 2, 8, NZ, NY, 16, 128), BF),
        pltpu.VMEM((PAIRS, 2, 8, NZ, NY, 16, 128), BF),
        pltpu.VMEM((SEQ, 16, 128), BF),
        pltpu.VMEM((SEQ, 16, 128), BF),
        pltpu.VMEM((SEQ, 16, 128), BF),
        pltpu.VMEM((PAIRS, SEQ, 3, 16, 128), BF),
        pltpu.VMEM((PAIRS, 2, 16, 128), BF),
        pltpu.VMEM((SEQ, 3, 16, 128), BF),
        pltpu.VMEM((SEQ, 3, 16, 128), BF),
        pltpu.VMEM((SEQ, 3, 16, 128), BF),
        pltpu.VMEM((EDGES, 16, 128), BF),
        pltpu.VMEM((EDGES, 16, 128), BF),
        pltpu.VMEM((EDGES, 16, 128), BF),
        pltpu.VMEM((PAIRS, 2, NZ, NY, 16, 128), BF),
        pltpu.VMEM((PAIRS, 2, NZ, NY, 16, 128), BF),
        pltpu.VMEM((PAIRS, 2, NZ, NY, 16, 128), BF),
        pltpu.VMEM((PAIRS, NY - 1, 2, 2, NZ, 16, 128), BF),
        pltpu.VMEM((PAIRS, 2, 2, NZ, 16, 128), BF),
        pltpu.VMEM((PAIRS, 2, NZ, 16, 128), BF),
        pltpu.VMEM((PAIRS, 2, NZ, 16, 128), BF),
        pltpu.VMEM((PAIRS, NZ - 1, 2, 16, 128), BF),
        pltpu.VMEM((PAIRS, SEQ, 16, 128), BF),
        pltpu.VMEM((PAIRS, 2, NZ, NY, 16, 128), BF),
        pltpu.VMEM((8, BLOCK, BLOCK), F32),
        pltpu.VMEM((8, BLOCK, BLOCK), BF),
        pltpu.VMEM((8, 128, BLOCK), BF),
        pltpu.VMEM((2, 8, 80, BLOCK), BF),
        pltpu.VMEM((2, 128, BLOCK), BF),
        pltpu.VMEM((2, BLOCK, 128), BF),
        pltpu.VMEM((128, BLOCK), F32),
        pltpu.VMEM((128, BLOCK), F32),
    ]
    dma = pltpu.SemaphoreType.DMA
    sems = [dma((PAIRS, 2)), dma((7 * PAIRS,))]
    sems += [dma((PAIRS,)) for _ in range(24)]
    sems += [dma((PAIRS, NY - 1)) for _ in range(2)] + [dma((PAIRS,)) for _ in range(2)]
    sems += [dma((PAIRS, NZ - 1)) for _ in range(2)] + [dma((PAIRS,)) for _ in range(2)]
    grid_rows = (NZ, NY, 16, PAIRS * 128)
    return pl.pallas_call(
        kernel,
        out_shape=tuple(jax.ShapeDtypeStruct((BLOCK, PAIRS * 128), BF) for _ in range(4)),
        in_specs=[smem, smem, smem, vmem, vmem, anywhere, anywhere],
        out_specs=(vmem,) * 4,
        scratch_shapes=scratch + sems,
        compiler_params=pltpu.CompilerParams(
            collective_id=0, has_side_effects=True, vmem_limit_bytes=60 * 1024 * 1024
        ),
    )(partners, inverse, global_blocks, queries, grad_output, key_states.reshape(grid_rows), value_states.reshape(grid_rows))


def solution(mesh):
    spec = P(("batch", "seq"), None)
    return jax.shard_map(
        step,
        mesh=mesh,
        in_specs=(spec, spec, spec, spec, P("batch", None), P("batch")),
        out_specs=(spec,) * 4,
        check_vma=False,
    )
```

```python
import functools
import math

import jax
import jax.numpy as jnp
from jax import lax
from jax.experimental import pallas as pl
from jax.experimental.pallas import tpu as pltpu
from jax.sharding import PartitionSpec as P

F32 = jnp.float32
BF = jnp.bfloat16
LOG2E = math.log2(math.e)
MESH = pl.DeviceIdType.MESH

PAIRS = 3
BLOCK = 512
SEQ = 64
NZ, NY = 8, 4
EDGES = 16
PARTS = ((0, 3), (3, 6), (6, 8))


def split(device):
    return device // 8, (device // 2) % 4, device % 2


def peers(me, start, stop, body):
    @pl.loop(start, stop)
    def _(k):
        body((me + k) % SEQ)


def remote(src, dst, send, recv, device):
    return pltpu.make_async_remote_copy(
        src_ref=src, dst_ref=dst, send_sem=send, recv_sem=recv, device_id={"seq": device}, device_id_type=MESH
    )


def local(src, dst, sem):
    return pltpu.make_async_copy(src, dst, sem)


def drain(ref, sem):
    pltpu.make_async_copy(ref, ref, sem).wait()


def edge_device(e):
    return (8 * (e // 2) + SEQ - 1 + e % 2) % SEQ


def edge_block(e):
    return (8 * (e // 2) + SEQ - e % 2) % SEQ


def rows(tiles):
    return tiles.reshape(BLOCK, 128)


def tiles(block):
    return block.reshape(NZ, NY, 16, 128)


def prepare(pair, q_ref, qt, qm):
    cols = slice(pair * 128, pair * 128 + 128)
    qs = q_ref[:, cols] * jnp.asarray(0.125, BF)
    lane = lax.broadcasted_iota(jnp.int32, (BLOCK, 128), 1)
    row = lax.broadcasted_iota(jnp.int32, (128, BLOCK), 0)
    qst = qs.T
    for h in range(2):
        qm[h] = jnp.where((lane >= 64) == (h == 1), qs, jnp.zeros_like(qs))
        qt[h] = jnp.where((row >= 64) == (h == 1), qst, jnp.zeros_like(qst))


def turn(pair, first, last, kv, kt, vt):
    @pl.loop(first, last)
    def _(j):
        kt[j] = rows(kv[pair, 0, j]).T
        t = rows(kv[pair, 1, j]).T
        for h in range(2):
            vt[h, j, 0:64] = t[64 * h : 64 * h + 64]
            vt[h, j, 64:80] = jnp.ones((16, BLOCK), BF)


def head(pair, h, gates, ticks, sends, kv, dkv, do_ref, ot, dqt, s_buf, p_buf, kt, vt, qt, qm):
    do_t = do_ref[:, pair * 128 : pair * 128 + 128].astype(F32).T
    qth = qt[h]

    def scores(j, peak):
        s = jnp.dot(rows(kv[pair, 0, j]), qth, preferred_element_type=F32)
        s_buf[j] = s
        return jnp.maximum(peak, jnp.max(s.reshape(BLOCK // 8, 8, BLOCK), axis=0))

    peak = jnp.full((8, BLOCK), -jnp.inf, F32)
    for gate, (first, last) in zip(gates, PARTS):
        gate(first, last)
        peak = lax.fori_loop(first, last, scores, peak)
    peak = jnp.max(peak, axis=0, keepdims=True) * LOG2E
    ticks[0]()

    def weigh(j, acc):
        p = jnp.exp2(s_buf[j] * LOG2E - peak).astype(BF)
        p_buf[j] = p
        return acc + jnp.dot(vt[h, j], p, preferred_element_type=F32)

    acc = lax.fori_loop(0, 8, weigh, jnp.zeros((80, BLOCK), F32))
    inverse = 1.0 / acc[64:65]
    out = acc[0:64] * inverse
    ot[64 * h : 64 * h + 64] = out
    do_n = (do_t[64 * h : 64 * h + 64] * inverse).astype(BF)
    dots = jnp.sum(do_n.astype(F32) * out, axis=0, keepdims=True)
    zero = jnp.zeros((64, BLOCK), BF)
    do_full = jnp.concatenate([do_n, zero] if h == 0 else [zero, do_n], axis=0)
    do_rows = do_full.T
    qmh = qm[h]
    ticks[1]()

    def backward(j, acc):
        p = p_buf[j]
        gw = jnp.dot(rows(kv[pair, 1, j]), do_full, preferred_element_type=F32)
        ds = (p.astype(F32) * (gw - dots)).astype(BF)
        dk = jnp.dot(ds, qmh, preferred_element_type=F32).astype(BF)
        dv = jnp.dot(p, do_rows, preferred_element_type=F32).astype(BF)
        if h == 0:
            dkv[pair, 0, j] = tiles(dk)
            dkv[pair, 1, j] = tiles(dv)
        else:
            dkv[pair, 0, j] = dkv[pair, 0, j] + tiles(dk)
            dkv[pair, 1, j] = dkv[pair, 1, j] + tiles(dv)
        return acc + jnp.dot(kt[j, 64 * h : 64 * h + 64], ds, preferred_element_type=F32)

    dq = jnp.zeros((64, BLOCK), F32)
    for send, (first, last) in zip(sends, PARTS[::-1]):
        dq = lax.fori_loop(first, last, backward, dq)
        send()
    dqt[64 * h : 64 * h + 64] = dq * 0.125


def kernel(
    table, inverse, shared_ids, q_ref, do_ref, k_ref, v_ref, o_ref, dq_ref, gk_ref, gv_ref,
    kv, dkv, spread0, spread1, spread2, picked, gsel, coming0, coming1, coming2, extra0, extra1, extra2, far_in, near_out, near_in,
    rsy, ysum, rsx, xsum, rsz, ret, retin,
    s_buf, p_buf, kt, vt, qt, qm, ot, dqt,
    load_sem, own_sem, p1_send, p1_recv, p2_send, p2_recv, na_send, na_recv, nf_send, nf_recv,
    gz_send, gz_recv, gx_send, gx_recv, gy_send, gy_recv,
    b1_send, b1_recv, bf_send, bf_recv, bn_send, bn_recv,
    pc_send, pc_recv, bc_send, bc_recv,
    ry_send, ry_recv, rx_send, rx_recv, rz_send, rz_recv, b2_send, b2_recv,
):
    spread = (spread0, spread1, spread2)
    coming = (coming0, coming1, coming2)
    extra = (extra0, extra1, extra2)
    me = lax.axis_index("seq")
    z, y, x = split(me)
    twin = z * 8 + y * 2 + 1 - x
    up = (me + 2) % SEQ
    down = (me + SEQ - 2) % SEQ
    ahead = up * (1 - x) + down * x
    behind = down * (1 - x) + up * x
    near = 2 - x
    far = 1 + x
    edge = y == 3 * x
    inner = y != 3 * x
    hands = y != 3 - 3 * x
    place = (2 * z + 1 + x) % EDGES

    def scoped(name):
        return jax.named_scope(name)

    def loads(pair):
        return [
            local(ref.at[:, :, :, pair * 128 : pair * 128 + 128], kv.at[pair, which, 0], load_sem.at[pair, which])
            for which, ref in enumerate((k_ref, v_ref))
        ]

    for pair in range(PAIRS):
        for copy in loads(pair):
            copy.start()

    barrier = pltpu.get_barrier_semaphore()

    def hello(device):
        pl.semaphore_signal(barrier, inc=1, device_id={"seq": device}, device_id_type=MESH)

    with scoped("barrier"):
        peers(me, 1, SEQ, hello)
        pl.semaphore_wait(barrier, SEQ - 1)

    def keep_own(pair):
        return local(kv.at[pair, x, 0, z, y], spread[pair].at[me], own_sem.at[pair])

    def keep(pair):
        for copy in loads(pair):
            copy.wait()
        keep_own(pair).start()

        def send(d):
            dz, dy, dx = split(d)
            remote(kv.at[pair, dx, 0, dz, dy], spread[pair].at[me], p1_send.at[pair], p1_recv.at[pair], d).start()

        peers(me, 1, SEQ, send)

    def kept(pair):
        keep_own(pair).wait()
        drain(spread[pair].at[pl.ds(0, SEQ - 1)], p1_recv.at[pair])

    def to_twin(pair):
        return remote(kv.at[pair, :, 0], kv.at[pair, :, 3 - near], na_send.at[pair], na_recv.at[pair], twin)

    def to_next(pair):
        return remote(kv.at[pair, :, near], kv.at[pair, :, 3 - near], nf_send.at[pair], nf_recv.at[pair], ahead)

    def hand_on(pair):
        to_twin(pair).wait_recv()

        @pl.when(hands)
        def _():
            to_next(pair).start()

    def edge_own(pair):
        mate = edge_block(place)
        return local(spread[pair].at[mate], kv.at[pair, x, far, z, y], own_sem.at[15 + pair])

    def edges(pair):
        @pl.loop(0, EDGES)
        def _(e):
            d = edge_device(e)

            @pl.when(d != me)
            def _():
                remote(
                    spread[pair].at[edge_block(e)], kv.at[pair, x, 2 - e % 2, z, y], pc_send.at[pair], pc_recv.at[pair], d
                ).start()

        @pl.when(edge)
        def _():
            edge_own(pair).start()

    def global_own(pair):
        return local(gsel.at[pair], kv.at[pair, x, 6:8, z, y], own_sem.at[3 + pair])

    def global_z(pair):
        for g in range(2):
            gsel[pair, g] = spread[pair][shared_ids[g]]
        global_own(pair).start()

        @pl.loop(1, 2 * NZ if pair == 0 else NZ)
        def _(k):
            d = plane(k) if pair == 0 else ((z + k) % NZ) * 8 + y * 2 + x
            remote(gsel.at[pair], kv.at[pair, x, 6:8, z, y], gz_send.at[pair], gz_recv.at[pair], d).start()

    def plane(k):
        return ((z + k // 2) % NZ) * 8 + y * 2 + (x + k) % 2

    def across(pair):
        return remote(
            kv.at[pair, x, 6:8, :, y], kv.at[pair, x, 6:8, :, y], gx_send.at[pair], gx_recv.at[pair], twin
        )

    def global_x(pair):
        global_own(pair).wait()
        drain(kv.at[pair, x, 6:8, 0 : NZ - 1, y], gz_recv.at[pair])
        across(pair).start()

    def global_y(pair):
        if pair == 0:
            global_own(pair).wait()
            drain(picked.at[pair, pl.ds(0, 10)], gz_recv.at[pair])
        else:
            across(pair).wait_recv()

        @pl.loop(1, NY)
        def _(k):
            d = z * 8 + ((y + k) % NY) * 2 + x
            remote(kv.at[pair, :, 6:8, :, y], kv.at[pair, :, 6:8, :, y], gy_send.at[pair], gy_recv.at[pair], d).start()

    def pick(pair):
        @pl.loop(0, SEQ)
        def _(d):
            for r in range(3):
                picked[pair, d, r] = spread[pair][table[r, d]]

    def route_own(pair):
        return local(picked.at[pair, me], kv.at[pair, x, 3:6, z, y], own_sem.at[6 + pair])

    def routes(pair):
        route_own(pair).start()

        def send(d):
            remote(picked.at[pair, d], kv.at[pair, x, 3:6, z, y], p2_send.at[pair], p2_recv.at[pair], d).start()

        peers(me, 1, SEQ, send)

    def arrive_near(pair):
        @pl.when(inner)
        def _():
            to_next(pair).wait_recv()

        @pl.when(edge)
        def _():
            edge_own(pair).wait()
            drain(spread[pair].at[pl.ds(0, SEQ - 1)], pc_recv.at[pair])

    def arrive_routes(pair):
        route_own(pair).wait()
        drain(picked.at[pair, pl.ds(0, SEQ - 1)], p2_recv.at[pair])

    def arrive_global(pair):
        drain(kv.at[pair, :, 6:8, :, 0 : NY - 1], gy_recv.at[pair])

    def back_far(pair):
        return remote(dkv.at[pair, :, far], far_in.at[pair], bf_send.at[pair], bf_recv.at[pair], behind)

    def back_near(pair):
        return remote(near_out.at[pair], near_in.at[pair], bn_send.at[pair], bn_recv.at[pair], twin)

    def back_own(pair):
        return local(dkv.at[pair, x, 3:6, z, y], coming[pair].at[me], own_sem.at[9 + pair])

    def ret_own(pair):
        return local(ret.at[pair, me], retin.at[pair, x, z, y], own_sem.at[12 + pair])

    def edge_back_own(pair):
        return local(dkv.at[pair, x, far, z, y], extra[pair].at[place], own_sem.at[18 + pair])

    def back_global(pair):
        for k in range(1, NY):
            to = (y + k) % NY
            remote(
                dkv.at[pair, :, 6:8, :, to], rsy.at[pair, k - 1], ry_send.at[pair, k - 1], ry_recv.at[pair, k - 1],
                z * 8 + to * 2 + x,
            ).start()

    def back_routes(pair):
        back_own(pair).start()

        def send(d):
            dz, dy, dx = split(d)
            remote(dkv.at[pair, dx, 3:6, dz, dy], coming[pair].at[me], b1_send.at[pair], b1_recv.at[pair], d).start()

        peers(me, 1, SEQ, send)

    def back_beyond(pair):
        @pl.when(inner)
        def _():
            back_far(pair).start()

        @pl.when(edge)
        def _():
            edge_back_own(pair).start()

            def send_edge(d):
                dz, dy, dx = split(d)
                remote(dkv.at[pair, dx, far, dz, dy], extra[pair].at[place], bc_send.at[pair], bc_recv.at[pair], d).start()

            peers(me, 1, SEQ, send_edge)

    def back_x(pair):
        return remote(ysum.at[pair, 1 - x], rsx.at[pair], rx_send.at[pair], rx_recv.at[pair], twin)

    def stage1(pair):
        for k in range(1, NY):
            drain(rsy.at[pair, k - 1], ry_recv.at[pair, k - 1])
        for which in range(2):
            total = dkv[pair, which, 6:8, :, y].astype(F32)
            for k in range(NY - 1):
                total = total + rsy[pair, k, which].astype(F32)
            ysum[pair, which] = total.astype(BF)
        back_x(pair).start()

    def relay(pair):
        @pl.when(hands)
        def _():
            back_far(pair).wait_recv()
            for which in range(2):
                total = dkv[pair, which, near].astype(F32) + far_in[pair, which].astype(F32)
                near_out[pair, which] = total.astype(BF)

        @pl.when(y == 3 - 3 * x)
        def _():
            for which in range(2):
                near_out[pair, which] = dkv[pair, which, near]

        back_near(pair).start()

    def stage2(pair):
        back_x(pair).wait_recv()
        xsum[pair] = (ysum[pair, x].astype(F32) + rsx[pair].astype(F32)).astype(BF)
        for k in range(1, NZ):
            to = (z + k) % NZ
            remote(
                xsum.at[pair, :, to], rsz.at[pair, k - 1], rz_send.at[pair, k - 1], rz_recv.at[pair, k - 1],
                to * 8 + y * 2 + x,
            ).start()

    def stage3(pair):
        for k in range(1, NZ):
            drain(rsz.at[pair, k - 1], rz_recv.at[pair, k - 1])
        shared = xsum[pair, :, z].astype(F32)
        for k in range(NZ - 1):
            shared = shared + rsz[pair, k].astype(F32)
        back_own(pair).wait()
        drain(coming[pair].at[pl.ds(0, SEQ - 1)], b1_recv.at[pair])

        @pl.when(edge)
        def _():
            edge_back_own(pair).wait()
            drain(extra[pair].at[pl.ds(0, EDGES - 1)], bc_recv.at[pair])

        @pl.when(inner)
        def _():
            drain(extra[pair], bc_recv.at[pair])

        def total_of(c):
            total = sum((shared_ids[g] == c).astype(F32) * shared[g] for g in range(2))
            for r in range(3):
                total = total + coming[pair][inverse[r, c], r].astype(F32)
            return total

        @pl.loop(0, SEQ)
        def _(c):
            ret[pair, c] = total_of(c).astype(BF)

        @pl.loop(0, EDGES)
        def _(e):
            c = edge_block(e)
            ret[pair, c] = (total_of(c) + extra[pair][e].astype(F32)).astype(BF)

        ret_own(pair).start()

        def send(d):
            remote(ret.at[pair, d], retin.at[pair, x, z, y], b2_send.at[pair], b2_recv.at[pair], d).start()

        peers(me, 1, SEQ, send)

    def stage4(pair):
        back_near(pair).wait_recv()
        ret_own(pair).wait()
        drain(ret.at[pair, pl.ds(0, SEQ - 1)], b2_recv.at[pair])
        for which, ref in enumerate((gk_ref, gv_ref)):
            total = dkv[pair, which, 0].astype(F32) + retin[pair, which].astype(F32) + near_in[pair, which].astype(F32)
            ref[:, pair * 128 : pair * 128 + 128] = rows(total.astype(BF))

    def finish(pair):
        cols = slice(pair * 128, pair * 128 + 128)
        o_ref[:, cols] = ot[...].T.astype(BF)
        dq_ref[:, cols] = dqt[...].T.astype(BF)

    def run(work):
        for stage, pair in work:
            with scoped("%s_%d" % (stage.__name__, pair)):
                stage(pair)

    def compute(pair, *work):
        prepare(pair, q_ref, qt, qm)

        def gated(arrive):
            def gate(first, last):
                run([(arrive, pair)])
                turn(pair, first, last, kv, kt, vt)

            return gate

        def nothing(*_):
            return None

        for h in range(2):
            ticks = [functools.partial(run, work[3 * h + i]) for i in range(3)]
            if h == 0:
                gates = [gated(arrive) for arrive in (arrive_near, arrive_routes, arrive_global)]
                sends = [nothing] * 3
            else:
                gates = [nothing] * 3
                sends = [functools.partial(run, [(stage, pair)]) for stage in (back_global, back_routes, back_beyond)]
            head(pair, h, gates, ticks, sends, kv, dkv, do_ref, ot, dqt, s_buf, p_buf, kt, vt, qt, qm)
            ticks[2]()
        finish(pair)

    def to_twin_start(pair):
        to_twin(pair).start()

    run([(keep, 0), (keep, 1), (keep, 2), (to_twin_start, 0), (to_twin_start, 1), (to_twin_start, 2)])
    run([(kept, 0), (global_z, 0), (kept, 1), (global_z, 1), (kept, 2), (global_z, 2), (pick, 0), (edges, 0), (routes, 0)])
    run([(hand_on, 0), (global_y, 0), (global_x, 1), (global_x, 2), (pick, 1), (pick, 2), (hand_on, 1)])
    run([(global_y, 1), (edges, 1), (routes, 1), (hand_on, 2)])
    compute(0, [(edges, 2), (routes, 2)], [(global_y, 2)], [], [], [], [])
    compute(1, [], [], [], [], [], [])
    compute(2, [(relay, 0)], [(stage1, 0)], [], [(stage2, 0), (stage1, 1)], [(relay, 1)], [(stage2, 1)])
    run([(stage3, 0), (stage1, 2), (stage3, 1), (stage2, 2), (relay, 2), (stage3, 2), (stage4, 0), (stage4, 1), (stage4, 2)])

    for pair in range(PAIRS):
        drain(spread[pair].at[pl.ds(0, SEQ - 1)], p1_send.at[pair])
        if pair == 0:
            drain(picked.at[pair, pl.ds(0, 10)], gz_send.at[pair])
        else:
            drain(kv.at[pair, x, 6:8, 0 : NZ - 1, y], gz_send.at[pair])
            across(pair).wait_send()
        for copy in (to_twin(pair), back_near(pair)):
            copy.wait_send()

        @pl.when(hands)
        def _():
            to_next(pair).wait_send()

        @pl.when(inner)
        def _():
            back_far(pair).wait_send()
            drain(extra[pair], pc_send.at[pair])

        @pl.when(edge)
        def _():
            drain(extra[pair].at[pl.ds(0, EDGES - 1)], pc_send.at[pair])
            drain(spread[pair].at[pl.ds(0, SEQ - 1)], bc_send.at[pair])

        drain(picked.at[pair, pl.ds(0, SEQ - 1)], p2_send.at[pair])
        drain(kv.at[pair, :, 6:8, :, 0 : NY - 1], gy_send.at[pair])
        drain(coming[pair].at[pl.ds(0, SEQ - 1)], b1_send.at[pair])
        for k in range(NY - 1):
            drain(rsy.at[pair, k], ry_send.at[pair, k])
        back_x(pair).wait_send()
        for k in range(NZ - 1):
            drain(rsz.at[pair, k], rz_send.at[pair, k])
        drain(ret.at[pair, pl.ds(0, SEQ - 1)], b2_send.at[pair])


def put(*refs):
    for src, dst in zip(refs[:4], refs[4:]):
        dst[...] = src[...]


def step(queries, key_states, value_states, grad_output, partners, global_blocks):
    ids = jnp.arange(SEQ, dtype=jnp.int32)
    inverse = jnp.sum(jnp.where(partners[:, :, None] == ids[None, None, :], ids[None, :, None], 0), axis=1)
    vmem = pl.BlockSpec(memory_space=pltpu.VMEM)
    smem = pl.BlockSpec(memory_space=pltpu.SMEM)
    anywhere = pl.BlockSpec(memory_space=pl.ANY)
    scratch = [
        pltpu.VMEM((PAIRS, 2, 8, NZ, NY, 16, 128), BF),
        pltpu.VMEM((PAIRS, 2, 8, NZ, NY, 16, 128), BF),
        pltpu.VMEM((SEQ, 16, 128), BF),
        pltpu.VMEM((SEQ, 16, 128), BF),
        pltpu.VMEM((SEQ, 16, 128), BF),
        pltpu.VMEM((PAIRS, SEQ, 3, 16, 128), BF),
        pltpu.VMEM((PAIRS, 2, 16, 128), BF),
        pltpu.VMEM((SEQ, 3, 16, 128), BF),
        pltpu.VMEM((SEQ, 3, 16, 128), BF),
        pltpu.VMEM((SEQ, 3, 16, 128), BF),
        pltpu.VMEM((EDGES, 16, 128), BF),
        pltpu.VMEM((EDGES, 16, 128), BF),
        pltpu.VMEM((EDGES, 16, 128), BF),
        pltpu.VMEM((PAIRS, 2, NZ, NY, 16, 128), BF),
        pltpu.VMEM((PAIRS, 2, NZ, NY, 16, 128), BF),
        pltpu.VMEM((PAIRS, 2, NZ, NY, 16, 128), BF),
        pltpu.VMEM((PAIRS, NY - 1, 2, 2, NZ, 16, 128), BF),
        pltpu.VMEM((PAIRS, 2, 2, NZ, 16, 128), BF),
        pltpu.VMEM((PAIRS, 2, NZ, 16, 128), BF),
        pltpu.VMEM((PAIRS, 2, NZ, 16, 128), BF),
        pltpu.VMEM((PAIRS, NZ - 1, 2, 16, 128), BF),
        pltpu.VMEM((PAIRS, SEQ, 16, 128), BF),
        pltpu.VMEM((PAIRS, 2, NZ, NY, 16, 128), BF),
        pltpu.VMEM((8, BLOCK, BLOCK), F32),
        pltpu.VMEM((8, BLOCK, BLOCK), BF),
        pltpu.VMEM((8, 128, BLOCK), BF),
        pltpu.VMEM((2, 8, 80, BLOCK), BF),
        pltpu.VMEM((2, 128, BLOCK), BF),
        pltpu.VMEM((2, BLOCK, 128), BF),
        pltpu.VMEM((128, BLOCK), F32),
        pltpu.VMEM((128, BLOCK), F32),
    ]
    dma = pltpu.SemaphoreType.DMA
    sems = [dma((PAIRS, 2)), dma((7 * PAIRS,))]
    sems += [dma((PAIRS,)) for _ in range(24)]
    sems += [dma((PAIRS, NY - 1)) for _ in range(2)] + [dma((PAIRS,)) for _ in range(2)]
    sems += [dma((PAIRS, NZ - 1)) for _ in range(2)] + [dma((PAIRS,)) for _ in range(2)]
    grid_rows = (NZ, NY, 16, PAIRS * 128)
    shapes = tuple(jax.ShapeDtypeStruct((BLOCK, PAIRS * 128), BF) for _ in range(4))
    results = pl.pallas_call(
        kernel,
        out_shape=shapes,
        in_specs=[smem, smem, smem, vmem, vmem, anywhere, anywhere],
        out_specs=(vmem,) * 4,
        scratch_shapes=scratch + sems,
        compiler_params=pltpu.CompilerParams(
            collective_id=0, has_side_effects=True, vmem_limit_bytes=60 * 1024 * 1024
        ),
    )(partners, inverse, global_blocks, queries, grad_output, key_states.reshape(grid_rows), value_states.reshape(grid_rows))
    return pl.pallas_call(put, out_shape=shapes, in_specs=[vmem] * 4, out_specs=(vmem,) * 4)(*results)


def solution(mesh):
    spec = P(("batch", "seq"), None)
    return jax.shard_map(
        step,
        mesh=mesh,
        in_specs=(spec, spec, spec, spec, P("batch", None), P("batch")),
        out_specs=(spec,) * 4,
        check_vma=False,
    )
```

```python
import functools
import math

import jax
import jax.numpy as jnp
from jax import lax
from jax.experimental import pallas as pl
from jax.experimental.pallas import tpu as pltpu
from jax.sharding import PartitionSpec as P

F32 = jnp.float32
BF = jnp.bfloat16
LOG2E = math.log2(math.e)
MESH = pl.DeviceIdType.MESH

PAIRS = 3
BLOCK = 512
SEQ = 64
NZ, NY = 8, 4
EDGES = 16
PARTS = ((0, 3), (3, 6), (6, 8))


def split(device):
    return device // 8, (device // 2) % 4, device % 2


def peers(me, start, stop, body):
    @pl.loop(start, stop)
    def _(k):
        body((me + k) % SEQ)


def remote(src, dst, send, recv, device):
    return pltpu.make_async_remote_copy(
        src_ref=src, dst_ref=dst, send_sem=send, recv_sem=recv, device_id={"seq": device}, device_id_type=MESH
    )


def local(src, dst, sem):
    return pltpu.make_async_copy(src, dst, sem)


def drain(ref, sem):
    pltpu.make_async_copy(ref, ref, sem).wait()


def edge_device(e):
    return (8 * (e // 2) + SEQ - 1 + e % 2) % SEQ


def edge_block(e):
    return (8 * (e // 2) + SEQ - e % 2) % SEQ


def rows(tiles):
    return tiles.reshape(BLOCK, 128)


def tiles(block):
    return block.reshape(NZ, NY, 16, 128)


def prepare(pair, q_ref, qt, qm):
    cols = slice(pair * 128, pair * 128 + 128)
    qs = q_ref[:, cols] * jnp.asarray(0.125, BF)
    lane = lax.broadcasted_iota(jnp.int32, (BLOCK, 128), 1)
    row = lax.broadcasted_iota(jnp.int32, (128, BLOCK), 0)
    qst = qs.T
    for h in range(2):
        qm[h] = jnp.where((lane >= 64) == (h == 1), qs, jnp.zeros_like(qs))
        qt[h] = jnp.where((row >= 64) == (h == 1), qst, jnp.zeros_like(qst))


def turn(pair, first, last, kv, kt, vt):
    @pl.loop(first, last)
    def _(j):
        kt[j] = rows(kv[pair, 0, j]).T
        t = rows(kv[pair, 1, j]).T
        for h in range(2):
            vt[h, j, 0:64] = t[64 * h : 64 * h + 64]
            vt[h, j, 64:80] = jnp.ones((16, BLOCK), BF)


def head(pair, h, gates, ticks, sends, kv, dkv, do_ref, ot, dqt, s_buf, p_buf, kt, vt, qt, qm):
    do_t = do_ref[:, pair * 128 : pair * 128 + 128].astype(F32).T
    qth = qt[h]

    def scores(j, peak):
        s = jnp.dot(rows(kv[pair, 0, j]), qth, preferred_element_type=F32)
        s_buf[j] = s
        return jnp.maximum(peak, jnp.max(s.reshape(BLOCK // 8, 8, BLOCK), axis=0))

    peak = jnp.full((8, BLOCK), -jnp.inf, F32)
    for gate, (first, last) in zip(gates, PARTS):
        gate(first, last)
        peak = lax.fori_loop(first, last, scores, peak)
    peak = jnp.max(peak, axis=0, keepdims=True) * LOG2E
    ticks[0]()

    def weigh(j, acc):
        p = jnp.exp2(s_buf[j] * LOG2E - peak).astype(BF)
        p_buf[j] = p
        return acc + jnp.dot(vt[h, j], p, preferred_element_type=F32)

    acc = lax.fori_loop(0, 8, weigh, jnp.zeros((80, BLOCK), F32))
    inverse = 1.0 / acc[64:65]
    out = acc[0:64] * inverse
    ot[64 * h : 64 * h + 64] = out
    do_n = (do_t[64 * h : 64 * h + 64] * inverse).astype(BF)
    dots = jnp.sum(do_n.astype(F32) * out, axis=0, keepdims=True)
    zero = jnp.zeros((64, BLOCK), BF)
    do_full = jnp.concatenate([do_n, zero] if h == 0 else [zero, do_n], axis=0)
    do_rows = do_full.T
    qmh = qm[h]
    ticks[1]()

    def backward(j, acc):
        p = p_buf[j]
        gw = jnp.dot(rows(kv[pair, 1, j]), do_full, preferred_element_type=F32)
        ds = (p.astype(F32) * (gw - dots)).astype(BF)
        dk = jnp.dot(ds, qmh, preferred_element_type=F32).astype(BF)
        dv = jnp.dot(p, do_rows, preferred_element_type=F32).astype(BF)
        if h == 0:
            dkv[pair, 0, j] = tiles(dk)
            dkv[pair, 1, j] = tiles(dv)
        else:
            dkv[pair, 0, j] = dkv[pair, 0, j] + tiles(dk)
            dkv[pair, 1, j] = dkv[pair, 1, j] + tiles(dv)
        return acc + jnp.dot(kt[j, 64 * h : 64 * h + 64], ds, preferred_element_type=F32)

    dq = jnp.zeros((64, BLOCK), F32)
    for send, (first, last) in zip(sends, PARTS[::-1]):
        dq = lax.fori_loop(first, last, backward, dq)
        send()
    dqt[64 * h : 64 * h + 64] = dq * 0.125


def kernel(
    table, inverse, shared_ids, q_ref, do_ref, k_ref, v_ref, o_ref, dq_ref, gk_ref, gv_ref,
    kv, dkv, spread0, spread1, spread2, picked, gsel, coming0, coming1, coming2, extra0, extra1, extra2, far_in, near_out, near_in,
    rsy, ysum, rsx, xsum, rsz, ret, retin,
    s_buf, p_buf, kt, vt, qt, qm, ot, dqt,
    load_sem, own_sem, p1_send, p1_recv, p2_send, p2_recv, na_send, na_recv, nf_send, nf_recv,
    gz_send, gz_recv, gx_send, gx_recv, gy_send, gy_recv,
    b1_send, b1_recv, bf_send, bf_recv, bn_send, bn_recv,
    pc_send, pc_recv, bc_send, bc_recv,
    ry_send, ry_recv, rx_send, rx_recv, rz_send, rz_recv, b2_send, b2_recv,
):
    spread = (spread0, spread1, spread2)
    coming = (coming0, coming1, coming2)
    extra = (extra0, extra1, extra2)
    me = lax.axis_index("seq")
    z, y, x = split(me)
    twin = z * 8 + y * 2 + 1 - x
    up = (me + 2) % SEQ
    down = (me + SEQ - 2) % SEQ
    ahead = up * (1 - x) + down * x
    behind = down * (1 - x) + up * x
    near = 2 - x
    far = 1 + x
    edge = y == 3 * x
    inner = y != 3 * x
    hands = y != 3 - 3 * x
    place = (2 * z + 1 + x) % EDGES

    def scoped(name):
        return jax.named_scope(name)

    def loads(pair):
        return [
            local(ref.at[:, :, :, pair * 128 : pair * 128 + 128], kv.at[pair, which, 0], load_sem.at[pair, which])
            for which, ref in enumerate((k_ref, v_ref))
        ]

    for pair in range(PAIRS):
        for copy in loads(pair):
            copy.start()

    barrier = pltpu.get_barrier_semaphore()

    def hello(device):
        pl.semaphore_signal(barrier, inc=1, device_id={"seq": device}, device_id_type=MESH)

    with scoped("barrier"):
        peers(me, 1, SEQ, hello)
        pl.semaphore_wait(barrier, SEQ - 1)

    def keep_own(pair):
        return local(kv.at[pair, x, 0, z, y], spread[pair].at[me], own_sem.at[pair])

    def keep(pair):
        for copy in loads(pair):
            copy.wait()
        keep_own(pair).start()

        def send(d):
            dz, dy, dx = split(d)
            remote(kv.at[pair, dx, 0, dz, dy], spread[pair].at[me], p1_send.at[pair], p1_recv.at[pair], d).start()

        peers(me, 1, SEQ, send)

    def kept(pair):
        keep_own(pair).wait()
        drain(spread[pair].at[pl.ds(0, SEQ - 1)], p1_recv.at[pair])

    def to_twin(pair):
        return remote(kv.at[pair, :, 0], kv.at[pair, :, 3 - near], na_send.at[pair], na_recv.at[pair], twin)

    def to_next(pair):
        return remote(kv.at[pair, :, near], kv.at[pair, :, 3 - near], nf_send.at[pair], nf_recv.at[pair], ahead)

    def hand_on(pair):
        to_twin(pair).wait_recv()

        @pl.when(hands)
        def _():
            to_next(pair).start()

    def edge_own(pair):
        mate = edge_block(place)
        return local(spread[pair].at[mate], kv.at[pair, x, far, z, y], own_sem.at[15 + pair])

    def edges(pair):
        @pl.loop(0, EDGES)
        def _(e):
            d = edge_device(e)

            @pl.when(d != me)
            def _():
                remote(
                    spread[pair].at[edge_block(e)], kv.at[pair, x, 2 - e % 2, z, y], pc_send.at[pair], pc_recv.at[pair], d
                ).start()

        @pl.when(edge)
        def _():
            edge_own(pair).start()

    def global_own(pair):
        return local(gsel.at[pair], kv.at[pair, x, 6:8, z, y], own_sem.at[3 + pair])

    def global_z(pair):
        for g in range(2):
            gsel[pair, g] = spread[pair][shared_ids[g]]
        global_own(pair).start()

        @pl.loop(1, 2 * NZ if pair == 0 else NZ)
        def _(k):
            d = plane(k) if pair == 0 else ((z + k) % NZ) * 8 + y * 2 + x
            remote(gsel.at[pair], kv.at[pair, x, 6:8, z, y], gz_send.at[pair], gz_recv.at[pair], d).start()

    def plane(k):
        return ((z + k // 2) % NZ) * 8 + y * 2 + (x + k) % 2

    def across(pair):
        return remote(
            kv.at[pair, x, 6:8, :, y], kv.at[pair, x, 6:8, :, y], gx_send.at[pair], gx_recv.at[pair], twin
        )

    def global_x(pair):
        global_own(pair).wait()
        drain(kv.at[pair, x, 6:8, 0 : NZ - 1, y], gz_recv.at[pair])
        across(pair).start()

    def global_y(pair):
        if pair == 0:
            global_own(pair).wait()
            drain(picked.at[pair, pl.ds(0, 10)], gz_recv.at[pair])
        else:
            across(pair).wait_recv()

        @pl.loop(1, NY)
        def _(k):
            d = z * 8 + ((y + k) % NY) * 2 + x
            remote(kv.at[pair, :, 6:8, :, y], kv.at[pair, :, 6:8, :, y], gy_send.at[pair], gy_recv.at[pair], d).start()

    def pick(pair):
        @pl.loop(0, SEQ)
        def _(d):
            for r in range(3):
                picked[pair, d, r] = spread[pair][table[r, d]]

    def route_own(pair):
        return local(picked.at[pair, me], kv.at[pair, x, 3:6, z, y], own_sem.at[6 + pair])

    def routes(pair):
        route_own(pair).start()

        def send(d):
            remote(picked.at[pair, d], kv.at[pair, x, 3:6, z, y], p2_send.at[pair], p2_recv.at[pair], d).start()

        peers(me, 1, SEQ, send)

    def arrive_near(pair):
        @pl.when(inner)
        def _():
            to_next(pair).wait_recv()

        @pl.when(edge)
        def _():
            edge_own(pair).wait()
            drain(spread[pair].at[pl.ds(0, SEQ - 1)], pc_recv.at[pair])

    def arrive_routes(pair):
        route_own(pair).wait()
        drain(picked.at[pair, pl.ds(0, SEQ - 1)], p2_recv.at[pair])

    def arrive_global(pair):
        drain(kv.at[pair, :, 6:8, :, 0 : NY - 1], gy_recv.at[pair])

    def back_far(pair):
        return remote(dkv.at[pair, :, far], far_in.at[pair], bf_send.at[pair], bf_recv.at[pair], behind)

    def back_near(pair):
        return remote(near_out.at[pair], near_in.at[pair], bn_send.at[pair], bn_recv.at[pair], twin)

    def back_own(pair):
        return local(dkv.at[pair, x, 3:6, z, y], coming[pair].at[me], own_sem.at[9 + pair])

    def ret_own(pair):
        return local(ret.at[pair, me], retin.at[pair, x, z, y], own_sem.at[12 + pair])

    def edge_back_own(pair):
        return local(dkv.at[pair, x, far, z, y], extra[pair].at[place], own_sem.at[18 + pair])

    def back_global(pair):
        for k in range(1, NY):
            to = (y + k) % NY
            remote(
                dkv.at[pair, :, 6:8, :, to], rsy.at[pair, k - 1], ry_send.at[pair, k - 1], ry_recv.at[pair, k - 1],
                z * 8 + to * 2 + x,
            ).start()

    def back_routes(pair):
        back_own(pair).start()

        def send(d):
            dz, dy, dx = split(d)
            remote(dkv.at[pair, dx, 3:6, dz, dy], coming[pair].at[me], b1_send.at[pair], b1_recv.at[pair], d).start()

        peers(me, 1, SEQ, send)

    def back_beyond(pair):
        @pl.when(inner)
        def _():
            back_far(pair).start()

        @pl.when(edge)
        def _():
            edge_back_own(pair).start()

            def send_edge(d):
                dz, dy, dx = split(d)
                remote(dkv.at[pair, dx, far, dz, dy], extra[pair].at[place], bc_send.at[pair], bc_recv.at[pair], d).start()

            peers(me, 1, SEQ, send_edge)

    def back_x(pair):
        return remote(ysum.at[pair, 1 - x], rsx.at[pair], rx_send.at[pair], rx_recv.at[pair], twin)

    def stage1(pair):
        for k in range(1, NY):
            drain(rsy.at[pair, k - 1], ry_recv.at[pair, k - 1])
        for which in range(2):
            total = dkv[pair, which, 6:8, :, y].astype(F32)
            for k in range(NY - 1):
                total = total + rsy[pair, k, which].astype(F32)
            ysum[pair, which] = total.astype(BF)
        back_x(pair).start()

    def relay(pair):
        @pl.when(hands)
        def _():
            back_far(pair).wait_recv()
            for which in range(2):
                total = dkv[pair, which, near].astype(F32) + far_in[pair, which].astype(F32)
                near_out[pair, which] = total.astype(BF)

        @pl.when(y == 3 - 3 * x)
        def _():
            for which in range(2):
                near_out[pair, which] = dkv[pair, which, near]

        back_near(pair).start()

    def stage2(pair):
        back_x(pair).wait_recv()
        xsum[pair] = (ysum[pair, x].astype(F32) + rsx[pair].astype(F32)).astype(BF)
        for k in range(1, NZ):
            to = (z + k) % NZ
            remote(
                xsum.at[pair, :, to], rsz.at[pair, k - 1], rz_send.at[pair, k - 1], rz_recv.at[pair, k - 1],
                to * 8 + y * 2 + x,
            ).start()

    def stage3(pair):
        for k in range(1, NZ):
            drain(rsz.at[pair, k - 1], rz_recv.at[pair, k - 1])
        shared = xsum[pair, :, z].astype(F32)
        for k in range(NZ - 1):
            shared = shared + rsz[pair, k].astype(F32)
        back_own(pair).wait()
        drain(coming[pair].at[pl.ds(0, SEQ - 1)], b1_recv.at[pair])

        @pl.when(edge)
        def _():
            edge_back_own(pair).wait()
            drain(extra[pair].at[pl.ds(0, EDGES - 1)], bc_recv.at[pair])

        @pl.when(inner)
        def _():
            drain(extra[pair], bc_recv.at[pair])

        def total_of(c):
            total = sum((shared_ids[g] == c).astype(F32) * shared[g] for g in range(2))
            for r in range(3):
                total = total + coming[pair][inverse[r, c], r].astype(F32)
            return total

        @pl.loop(0, SEQ)
        def _(c):
            ret[pair, c] = total_of(c).astype(BF)

        @pl.loop(0, EDGES)
        def _(e):
            c = edge_block(e)
            ret[pair, c] = (total_of(c) + extra[pair][e].astype(F32)).astype(BF)

        ret_own(pair).start()

        def send(d):
            remote(ret.at[pair, d], retin.at[pair, x, z, y], b2_send.at[pair], b2_recv.at[pair], d).start()

        peers(me, 1, SEQ, send)

    def stage4(pair):
        back_near(pair).wait_recv()
        ret_own(pair).wait()
        drain(ret.at[pair, pl.ds(0, SEQ - 1)], b2_recv.at[pair])
        for which, ref in enumerate((gk_ref, gv_ref)):
            total = dkv[pair, which, 0].astype(F32) + retin[pair, which].astype(F32) + near_in[pair, which].astype(F32)
            ref[:, pair * 128 : pair * 128 + 128] = rows(total.astype(BF))

    def finish(pair):
        cols = slice(pair * 128, pair * 128 + 128)
        o_ref[:, cols] = ot[...].T.astype(BF)
        dq_ref[:, cols] = dqt[...].T.astype(BF)

    def run(work):
        for stage, pair in work:
            with scoped("%s_%d" % (stage.__name__, pair)):
                stage(pair)

    def compute(pair, *work):
        prepare(pair, q_ref, qt, qm)

        def gated(arrive):
            def gate(first, last):
                run([(arrive, pair)])
                turn(pair, first, last, kv, kt, vt)

            return gate

        def nothing(*_):
            return None

        for h in range(2):
            ticks = [functools.partial(run, work[3 * h + i]) for i in range(3)]
            if h == 0:
                gates = [gated(arrive) for arrive in (arrive_near, arrive_routes, arrive_global)]
                sends = [nothing] * 3
            else:
                gates = [nothing] * 3
                sends = [functools.partial(run, [(stage, pair)]) for stage in (back_global, back_routes, back_beyond)]
            head(pair, h, gates, ticks, sends, kv, dkv, do_ref, ot, dqt, s_buf, p_buf, kt, vt, qt, qm)
            ticks[2]()
        finish(pair)

    def to_twin_start(pair):
        to_twin(pair).start()

    run([(keep, 0), (keep, 1), (keep, 2), (to_twin_start, 0), (to_twin_start, 1), (to_twin_start, 2)])
    run([(kept, 0), (global_z, 0), (kept, 1), (global_z, 1), (kept, 2), (global_z, 2), (pick, 0), (edges, 0), (routes, 0)])
    run([(hand_on, 0), (pick, 1), (edges, 1), (global_y, 0), (routes, 1), (global_x, 1), (global_x, 2)])
    run([(hand_on, 1), (hand_on, 2), (pick, 2), (global_y, 1)])
    compute(0, [(edges, 2), (routes, 2)], [(global_y, 2)], [], [], [], [])
    compute(1, [], [], [], [], [], [])
    compute(2, [(relay, 0)], [(stage1, 0)], [], [(stage2, 0), (stage1, 1)], [(relay, 1)], [(stage2, 1)])
    run([(stage3, 0), (stage1, 2), (stage3, 1), (stage2, 2), (relay, 2), (stage3, 2), (stage4, 0), (stage4, 1), (stage4, 2)])

    for pair in range(PAIRS):
        drain(spread[pair].at[pl.ds(0, SEQ - 1)], p1_send.at[pair])
        if pair == 0:
            drain(picked.at[pair, pl.ds(0, 10)], gz_send.at[pair])
        else:
            drain(kv.at[pair, x, 6:8, 0 : NZ - 1, y], gz_send.at[pair])
            across(pair).wait_send()
        for copy in (to_twin(pair), back_near(pair)):
            copy.wait_send()

        @pl.when(hands)
        def _():
            to_next(pair).wait_send()

        @pl.when(inner)
        def _():
            back_far(pair).wait_send()
            drain(extra[pair], pc_send.at[pair])

        @pl.when(edge)
        def _():
            drain(extra[pair].at[pl.ds(0, EDGES - 1)], pc_send.at[pair])
            drain(spread[pair].at[pl.ds(0, SEQ - 1)], bc_send.at[pair])

        drain(picked.at[pair, pl.ds(0, SEQ - 1)], p2_send.at[pair])
        drain(kv.at[pair, :, 6:8, :, 0 : NY - 1], gy_send.at[pair])
        drain(coming[pair].at[pl.ds(0, SEQ - 1)], b1_send.at[pair])
        for k in range(NY - 1):
            drain(rsy.at[pair, k], ry_send.at[pair, k])
        back_x(pair).wait_send()
        for k in range(NZ - 1):
            drain(rsz.at[pair, k], rz_send.at[pair, k])
        drain(ret.at[pair, pl.ds(0, SEQ - 1)], b2_send.at[pair])


def put(*refs):
    buffers, load_sem, store_sem = refs[8:]
    loads = [local(refs[i], buffers.at[i], load_sem.at[i]) for i in range(4)]
    stores = [local(buffers.at[i], refs[4 + i], store_sem.at[i]) for i in range(4)]
    for copy in loads:
        copy.start()
    for load, store in zip(loads, stores):
        load.wait()
        store.start()
    for copy in stores:
        copy.wait()


def step(queries, key_states, value_states, grad_output, partners, global_blocks):
    ids = jnp.arange(SEQ, dtype=jnp.int32)
    inverse = jnp.sum(jnp.where(partners[:, :, None] == ids[None, None, :], ids[None, :, None], 0), axis=1)
    vmem = pl.BlockSpec(memory_space=pltpu.VMEM)
    smem = pl.BlockSpec(memory_space=pltpu.SMEM)
    anywhere = pl.BlockSpec(memory_space=pl.ANY)
    scratch = [
        pltpu.VMEM((PAIRS, 2, 8, NZ, NY, 16, 128), BF),
        pltpu.VMEM((PAIRS, 2, 8, NZ, NY, 16, 128), BF),
        pltpu.VMEM((SEQ, 16, 128), BF),
        pltpu.VMEM((SEQ, 16, 128), BF),
        pltpu.VMEM((SEQ, 16, 128), BF),
        pltpu.VMEM((PAIRS, SEQ, 3, 16, 128), BF),
        pltpu.VMEM((PAIRS, 2, 16, 128), BF),
        pltpu.VMEM((SEQ, 3, 16, 128), BF),
        pltpu.VMEM((SEQ, 3, 16, 128), BF),
        pltpu.VMEM((SEQ, 3, 16, 128), BF),
        pltpu.VMEM((EDGES, 16, 128), BF),
        pltpu.VMEM((EDGES, 16, 128), BF),
        pltpu.VMEM((EDGES, 16, 128), BF),
        pltpu.VMEM((PAIRS, 2, NZ, NY, 16, 128), BF),
        pltpu.VMEM((PAIRS, 2, NZ, NY, 16, 128), BF),
        pltpu.VMEM((PAIRS, 2, NZ, NY, 16, 128), BF),
        pltpu.VMEM((PAIRS, NY - 1, 2, 2, NZ, 16, 128), BF),
        pltpu.VMEM((PAIRS, 2, 2, NZ, 16, 128), BF),
        pltpu.VMEM((PAIRS, 2, NZ, 16, 128), BF),
        pltpu.VMEM((PAIRS, 2, NZ, 16, 128), BF),
        pltpu.VMEM((PAIRS, NZ - 1, 2, 16, 128), BF),
        pltpu.VMEM((PAIRS, SEQ, 16, 128), BF),
        pltpu.VMEM((PAIRS, 2, NZ, NY, 16, 128), BF),
        pltpu.VMEM((8, BLOCK, BLOCK), F32),
        pltpu.VMEM((8, BLOCK, BLOCK), BF),
        pltpu.VMEM((8, 128, BLOCK), BF),
        pltpu.VMEM((2, 8, 80, BLOCK), BF),
        pltpu.VMEM((2, 128, BLOCK), BF),
        pltpu.VMEM((2, BLOCK, 128), BF),
        pltpu.VMEM((128, BLOCK), F32),
        pltpu.VMEM((128, BLOCK), F32),
    ]
    dma = pltpu.SemaphoreType.DMA
    sems = [dma((PAIRS, 2)), dma((7 * PAIRS,))]
    sems += [dma((PAIRS,)) for _ in range(24)]
    sems += [dma((PAIRS, NY - 1)) for _ in range(2)] + [dma((PAIRS,)) for _ in range(2)]
    sems += [dma((PAIRS, NZ - 1)) for _ in range(2)] + [dma((PAIRS,)) for _ in range(2)]
    grid_rows = (NZ, NY, 16, PAIRS * 128)
    shapes = tuple(jax.ShapeDtypeStruct((BLOCK, PAIRS * 128), BF) for _ in range(4))
    results = pl.pallas_call(
        kernel,
        out_shape=shapes,
        in_specs=[smem, smem, smem, vmem, vmem, anywhere, anywhere],
        out_specs=(vmem,) * 4,
        scratch_shapes=scratch + sems,
        compiler_params=pltpu.CompilerParams(
            collective_id=0, has_side_effects=True, vmem_limit_bytes=60 * 1024 * 1024
        ),
    )(partners, inverse, global_blocks, queries, grad_output, key_states.reshape(grid_rows), value_states.reshape(grid_rows))
    return pl.pallas_call(
        put,
        out_shape=shapes,
        in_specs=[anywhere] * 4,
        out_specs=(anywhere,) * 4,
        scratch_shapes=[pltpu.VMEM((4, BLOCK, PAIRS * 128), BF), dma((4,)), dma((4,))],
    )(*results)


def solution(mesh):
    spec = P(("batch", "seq"), None)
    return jax.shard_map(
        step,
        mesh=mesh,
        in_specs=(spec, spec, spec, spec, P("batch", None), P("batch")),
        out_specs=(spec,) * 4,
        check_vma=False,
    )
```
